256 devices in a mesh: chan: 16 (over y_lo, x, core), space: 16 (over y_hi, z).
Axes of the slice: x: 4, y: 4 (y_hi: 2, y_lo: 2; y = y_hi * 2 + y_lo), z: 8, core: 2. Of those that a mesh axis runs over, the one named last changes fastest.
Arguments:
- features: bfloat16 [256, 2, 128, 64], P('chan', None, 'space'), may hold values from -6 to 6
- weights: bfloat16 [4, 4, 4, 256, 128], P(None, None, None, None, 'chan'), may hold values from -0.1875 to 0.1875
- cotangent: bfloat16 [128, 4, 256, 128], P('chan', None, 'space'), may hold values from -6 to 6
Outputs:
- decoded: bfloat16 [128, 4, 256, 128], P('chan', None, 'space')
- input_grad: bfloat16 [256, 2, 128, 64], P('chan', None, 'space')
The draws below stay inside these ranges and needn't reach their ends.
All inputs are finite; a program needn't handle non-finite values.
Results may differ from the reference program's by a relative error of at most 0.0012.
Values may be sent and summed in bfloat16 or wider, within the bound.
No kernel may reach another device: no remote copies, remote signals or barrier semaphores. Data moves between devices by JAX's collectives and lax.ppermute only.
A program may use at most 64 MiB of HBM per device.

```python
import jax
import jax.numpy as jnp
from jax import lax

CIN = 256
COUT = 128
KS = 4
PX = 2
PZ = 64
NY = 128


def with_spikes(result, key, source, target, blocks, factor):
    owner, partner = [(jnp.arange(result.shape[position]) // (result.shape[position] // blocks)).reshape([-1 if axis == position else 1 for axis in range(result.ndim)]) for position in (source, target)]
    chosen = jax.random.permutation(key, blocks)[partner]
    strong = (owner == chosen) | (owner == (partner + blocks // 2) % blocks)
    return jnp.where(strong, factor * result, result)


def level_of(rng, extent, cuts, low, top_value):
    level = 1.0
    for axis_at, shards_of in cuts:
        draws = jax.random.uniform(jax.random.fold_in(jax.random.fold_in(rng, 6), axis_at), (shards_of,), jnp.float32, low / len(cuts), top_value / len(cuts))
        level = level * jnp.repeat(jnp.exp(draws), extent[axis_at] // shards_of).reshape((-1,) + (1,) * (len(extent) - 1 - axis_at))
    return level


def noise(own_key, extent, deviation, most, cuts=(), dtype=jnp.bfloat16):
    loudness = level_of(own_key, extent, cuts, -0.22, 0.18) if cuts else 1.0
    drawn = jax.random.normal(own_key, extent, jnp.float32) * deviation * loudness
    return jnp.minimum(jnp.maximum(drawn, -most), most).astype(dtype)


def gaussian_with(own_key, extent, scale, limit, split, heavy, kind=jnp.bfloat16):
    array = scale * jax.random.normal(own_key, extent, jnp.float32)
    if split:
        array = array * level_of(own_key, extent, split, -0.22, 0.18)
    return jnp.clip(with_spikes(array, jax.random.fold_in(own_key, 3), *heavy), -limit, limit).astype(kind)


def setup_inputs(seed: int = 0) -> dict:
    keys = jax.random.split(jax.random.key(seed), 4)
    features = noise(keys[0], (CIN, PX, NY, PZ), 1.0, 6.0, ((0, 16), (2, 16)))
    weights = gaussian_with(keys[1], (KS, KS, KS, CIN, COUT), (CIN * 8) ** -0.5, 0.1875, ((4, 16),), (4, 3, 16, 2.0))
    cotangent = noise(keys[2], (COUT, 2 * PX, 2 * NY, 2 * PZ), 1.0, 6.0, ((0, 16), (2, 16)))
    return {"features": features, "weights": weights, "cotangent": cotangent}


def reference(features, weights, cotangent):
    kernel_flip = jnp.flip(weights, (0, 1, 2))
    forward = lax.conv_general_dilated(
        features[None], kernel_flip, (1, 1, 1), ((2, 2), (2, 2), (2, 2)),
        lhs_dilation=(2, 2, 2), dimension_numbers=("NCDHW", "DHWIO", "NCDHW"),
        preferred_element_type=jnp.float32)
    decoded = forward[0].astype(jnp.bfloat16)
    backward = lax.conv_general_dilated(
        cotangent[None], weights, (2, 2, 2), ((1, 1), (1, 1), (1, 1)),
        dimension_numbers=("NCDHW", "DHWOI", "NCDHW"),
        preferred_element_type=jnp.float32)
    input_grad = backward[0].astype(jnp.bfloat16)
    return decoded, input_grad
```

```python
import jax
import jax.numpy as jnp
from jax import lax
from jax.experimental import pallas as pl
from jax.experimental.pallas import tpu as pltpu
from jax.sharding import PartitionSpec as P

BF = jnp.bfloat16
F32 = jnp.float32


def call(body, outs, scratch, cost):
    return pl.pallas_call(
        body,
        out_shape=outs,
        scratch_shapes=scratch,
        cost_estimate=pl.CostEstimate(flops=cost[0], bytes_accessed=cost[1], transcendentals=0),
    )


def dot(a, b, dims=((1,), (0,))):
    return lax.dot_general(a, b, (dims, ((), ())), preferred_element_type=F32)


def core_index():
    return lax.rem(lax.axis_index("chan"), 2)


def pack_body(feat, cot, flat, turned, edge_a, edge_b, fs, cs):
    for ch in range(16):
        for u in range(2):
            fs[pl.ds(ch * 16 + u * 8, 8), :] = feat[ch, u].astype(F32)
    for o in range(8):
        for a in range(4):
            cs[pl.ds((o * 4 + a) * 16, 16), :] = cot[o, a].astype(F32)
    tiles = []
    for v in range(8):
        tile = jnp.concatenate([fs[pl.ds(v, 16, stride=16), :], fs[pl.ds(8 + v, 16, stride=16), :]], axis=1)
        tiles.append(tile)
        flat[:, v * 128 : (v + 1) * 128] = tile.astype(BF)
    firsts, lasts = [], []
    for a in range(4):
        for b in range(0, 16, 2):
            lo = cs[pl.ds(a * 16 + b, 8, stride=64), :]
            hi = cs[pl.ds(a * 16 + b + 1, 8, stride=64), :]
            turned[pl.ds((a * 16 + b) * 8, 16), :] = jnp.concatenate([lo, hi], axis=0).astype(BF)
            if b == 0:
                firsts.append(lo)
            if b == 14:
                lasts.append(hi)
    first = jnp.concatenate([tiles[0]] + firsts, axis=0)
    last = jnp.concatenate([tiles[7]] + lasts, axis=0)
    core = jnp.full(first.shape, core_index(), jnp.int32)
    edge_a[...] = jnp.where(core == 0, last, first).astype(BF)
    edge_b[...] = jnp.where(core == 0, first, last).astype(BF)


def pack(feat, cot):
    s = jax.ShapeDtypeStruct
    return call(
        pack_body,
        (s((16, 1024), BF), s((512, 128), BF), s((48, 128), BF), s((48, 128), BF)),
        [pltpu.VMEM((256, 64), F32), pltpu.VMEM((512, 128), F32)],
        (0, 400000),
    )(feat, cot)


def grad_body(w_own, w_other, c_own, c_other, h_own, h_other, out, rows, cols, wk):
    core = core_index()
    i = lax.broadcasted_iota(jnp.int32, (256, 512), 0)
    j = lax.broadcasted_iota(jnp.int32, (256, 512), 1)
    c = lax.rem(i, 128)
    want = 2 * lax.rem(j, 64) + lax.div(j, 128) - 1
    same = lax.div(i, 128) == lax.rem(lax.div(j, 64), 2)
    select = jnp.where((c == want) & same, 1.0, 0.0).astype(BF)
    zero = jnp.zeros((80, 128), BF)
    for k, (w_ref, c_ref, h_ref) in enumerate(((w_own, c_own, h_own), (w_other, c_other, h_other))):
        for a in range(4):
            @pl.when(core == 0)
            def _():
                rows[k, a, 0:8, :] = h_ref[16 + 8 * a : 24 + 8 * a, :].astype(F32)
                rows[k, a, 8:80, :] = c_ref[a * 128 : a * 128 + 72, :].astype(F32)

            @pl.when(core == 1)
            def _():
                rows[k, a, 0:72, :] = c_ref[a * 128 + 56 : a * 128 + 128, :].astype(F32)
                rows[k, a, 72:80, :] = h_ref[16 + 8 * a : 24 + 8 * a, :].astype(F32)
        plane = [rows[k, a].astype(BF) for a in range(4)]
        for p in range(4):
            low = plane[p - 1] if p > 0 else zero
            high = plane[p + 1] if p < 3 else zero
            cols[k, p] = dot(jnp.concatenate([low, high], axis=1), select).astype(BF)
            for r in range(4):
                taps = [w_ref[p, q, r].astype(F32) for q in range(4)]
                wk[pl.ds(((k * 4 + p) * 4 + r) * 32, 32), :] = jnp.concatenate(taps, axis=0).astype(BF)
    wt = wk[...].T
    for pair in range(2):
        halves = []
        for v in (2 * pair, 2 * pair + 1):
            parts = [
                cols[k, p, 16 * v : 16 * v + 32, r * 128 : (r + 1) * 128]
                for k in range(2)
                for p in range(4)
                for r in range(4)
            ]
            halves.append(jnp.concatenate(parts, axis=0))
        out[:, pair * 256 : (pair + 1) * 256] = dot(wt, jnp.concatenate(halves, axis=1))


def grad(w_own, w_other, c_own, c_other, h_own, h_other):
    return call(
        grad_body,
        jax.ShapeDtypeStruct((256, 512), F32),
        [pltpu.VMEM((2, 4, 80, 128), F32), pltpu.VMEM((2, 4, 80, 512), BF), pltpu.VMEM((1024, 256), BF)],
        (500000000, 1400000),
    )(w_own, w_other, c_own, c_other, h_own, h_other)


def total_body(parts, out, rows):
    for half in range(2):
        acc = parts[half]
        for chip in range(1, 8):
            acc = acc + parts[2 * chip + half]
        for k in range(4):
            v = 4 * half + k
            for u in range(2):
                rows[pl.ds(u * 8 + v, 16, stride=16), :] = acc[:, k * 128 + u * 64 : k * 128 + (u + 1) * 64]
    for ch in range(16):
        for u in range(2):
            out[ch, u] = rows[pl.ds(ch * 16 + u * 8, 8), :].astype(BF)


def total(parts):
    return call(
        total_body,
        jax.ShapeDtypeStruct((16, 2, 8, 64), BF),
        [pltpu.VMEM((256, 64), F32)],
        (200000, 600000),
    )(parts)


def up_body(weights, own, other, out, f, y, fine):
    core = core_index()
    mine = pl.multiple_of(core * 16, 16)
    theirs = pl.multiple_of(16 - core * 16, 16)
    side, far = core * 9, 9 - core * 9
    for chip in range(8):
        a = pl.ds(pl.multiple_of(chip * 32 + mine, 16), 16)
        b = pl.ds(pl.multiple_of(chip * 32 + theirs, 16), 16)
        for v in range(8):
            f[v + 1, a, :] = own[chip, :, v * 128 : (v + 1) * 128]
            f[v + 1, b, :] = other[chip, :, v * 128 : (v + 1) * 128]
        f[side, a, :] = own[chip, :, 1024:1152]
        f[side, b, :] = own[chip, :, 1152:1280]
        f[far, b, :] = other[chip, :, 1024:1152]
        f[far, a, :] = other[chip, :, 1152:1280]
    w = weights[...]
    for t in range(5):
        y[t] = dot(w, jnp.concatenate([f[2 * t], f[2 * t + 1]], axis=1))

    def tap(p, q, r, v):
        t = v + 1
        return y[t // 2, pl.ds(((p * 4 + q) * 4 + r) * 8, 8), (t % 2) * 128 : (t % 2 + 1) * 128]

    lane = lax.broadcasted_iota(jnp.int32, (8, 128), 1)
    first_half = lane < 64
    cell = lax.rem(lane, 64)
    ii = lax.broadcasted_iota(jnp.int32, (256, 256), 0)
    jj = lax.broadcasted_iota(jnp.int32, (256, 256), 1)
    spread = jnp.where(
        (lax.div(jj, 128) == lax.rem(lax.div(ii, 64), 2))
        & (lax.rem(jj, 128) == 2 * lax.rem(ii, 64) + lax.div(ii, 128)),
        1.0,
        0.0,
    ).astype(BF)
    for pb in range(2):
        blocks = {0: [], 1: []}
        for n in range(8):
            pairs = ((1, n), (3, n - 1)) if pb == 0 else ((2, n), (0, n + 1))
            got = {0: [], 1: []}
            for r in range(4):
                s = [sum(tap(p, q, r, v) for q, v in pairs) for p in range(4)]
                moved = pltpu.roll(jnp.where(first_half, s[3], s[0]), 64, 1)
                got[0].append(s[1] + jnp.where(first_half, 0.0, moved))
                got[1].append(s[2] + jnp.where(first_half, moved, 0.0))
            for pa in range(2):
                t0, t1, t2, t3 = got[pa]
                even = t1 + jnp.where(cell == 0, 0.0, pltpu.roll(t3, 1, 1))
                odd = t2 + jnp.where(cell == 63, 0.0, pltpu.roll(t0, 127, 1))
                blocks[pa].append(jnp.concatenate([even, odd], axis=1))
        for pa in range(2):
            rows = dot(jnp.concatenate(blocks[pa], axis=0).astype(BF), spread)
            for n in range(8):
                for m in range(2):
                    fine[pl.ds((2 * m + pa) * 16 + 2 * n + pb, 8, stride=64), :] = rows[
                        n * 8 : (n + 1) * 8, m * 128 : (m + 1) * 128
                    ]
    for o in range(8):
        for a in range(4):
            out[o, a] = fine[pl.ds((o * 4 + a) * 16, 16), :].astype(BF)


def upsample(weights, own, other):
    return call(
        up_body,
        jax.ShapeDtypeStruct((8, 4, 16, 128), BF),
        [pltpu.VMEM((10, 256, 128), BF), pltpu.VMEM((5, 512, 256), F32), pltpu.VMEM((512, 128), F32)],
        (400000000, 1100000),
    )(weights, own, other)


def local(features, weights, cotangent):
    tiles = lax.axis_size("space")
    chans = lax.axis_size("chan")
    at = lambda ch, sp: ch * tiles + sp
    swap = [(ch, ch ^ 1) for ch in range(chans)]
    cross_a, cross_b = [], []
    for ch in range(chans):
        for sp in range(tiles):
            if ch % 2 == 0:
                if sp + 1 < tiles:
                    cross_a.append((at(ch, sp), at(ch, sp + 1)))
                    cross_b.append((at(ch + 1, sp), at(ch, sp + 1)))
            elif sp > 0:
                cross_a.append((at(ch, sp), at(ch, sp - 1)))
                cross_b.append((at(ch - 1, sp), at(ch, sp - 1)))
    both = ("chan", "space")
    by_core = [[2 * chip + core for chip in range(chans // 2)] for core in range(2)]

    w_own = jnp.transpose(weights, (0, 1, 2, 4, 3))
    w_other = lax.ppermute(w_own, "chan", swap)
    flat, turned, edge_a, edge_b = pack(features, cotangent)
    turned_other = lax.ppermute(turned, "chan", swap)
    halo_a = lax.ppermute(edge_a, both, cross_a)
    halo_b = lax.ppermute(edge_b, both, cross_b)

    block = jnp.concatenate([flat, halo_a[:16], halo_b[:16]], axis=1)
    copies = jnp.broadcast_to(block[None], (8, 16, 1280))
    own = lax.all_to_all(copies, "chan", 0, 0, tiled=True, axis_index_groups=by_core)

    partial = grad(w_own, w_other, turned, turned_other, halo_a, halo_b)
    pieces = lax.all_to_all(partial.reshape(16, 16, 512), "chan", 0, 0, tiled=True)

    other = lax.ppermute(own, "chan", swap)
    decoded = upsample(w_own.reshape(512, 256), own, other)
    return decoded, total(pieces)


def solution(mesh):
    return jax.shard_map(
        local,
        mesh=mesh,
        in_specs=(
            P("chan", None, "space", None),
            P(None, None, None, None, "chan"),
            P("chan", None, "space", None),
        ),
        out_specs=(P("chan", None, "space", None), P("chan", None, "space", None)),
        check_vma=False,
    )
```

```python
import jax
import jax.numpy as jnp
from jax import lax
from jax.experimental import pallas as pl
from jax.experimental.pallas import tpu as pltpu
from jax.sharding import PartitionSpec as P

BF = jnp.bfloat16
F32 = jnp.float32


def s(shape, kind=BF):
    return jax.ShapeDtypeStruct(shape, kind)


def call(body, outs, scratch, cost, **kw):
    return pl.pallas_call(
        body,
        out_shape=outs,
        scratch_shapes=scratch,
        cost_estimate=pl.CostEstimate(flops=cost[0], bytes_accessed=cost[1], transcendentals=0),
        compiler_params=pltpu.CompilerParams(vmem_limit_bytes=12 * 1024 * 1024),
        **kw,
    )


def dot(a, b, dims=((1,), (0,))):
    return lax.dot_general(a, b, (dims, ((), ())), preferred_element_type=F32)


def core_index():
    return lax.rem(lax.axis_index("chan"), 2)


def pick(core, zero, one):
    return jnp.where(jnp.full(zero.shape, core, jnp.int32) == 0, zero, one)


def cell_rows(feat, fs, rows):
    for ch in range(16):
        for u in range(2):
            fs[pl.ds(ch * 16 + u * 8, 8), :] = feat[ch, u].astype(F32)
    return {
        v: jnp.concatenate([fs[pl.ds(v, 16, stride=16), :], fs[pl.ds(8 + v, 16, stride=16), :]], axis=1)
        for v in rows
    }


def fine_rows(cot, cs):
    for o in range(8):
        for a in range(4):
            cs[pl.ds((o * 4 + a) * 16, 16), :] = cot[o, a].astype(F32)


def half_rows(cs, core, out):
    for a in range(4):
        for n in range(9):
            near = cs[pl.ds(a * 16 + n, 8, stride=64), :]
            far = cs[pl.ds(a * 16 + n + 7, 8, stride=64), :]
            out[a, n * 8 : (n + 1) * 8, :] = pick(core, near, far)


def edge_rows(tiles, cs, core):
    first = jnp.concatenate([tiles[0]] + [cs[pl.ds(a * 16, 8, stride=64), :] for a in range(4)], axis=0)
    last = jnp.concatenate([tiles[7]] + [cs[pl.ds(a * 16 + 15, 8, stride=64), :] for a in range(4)], axis=0)
    return pick(core, last, first)


def turned_weights(w, wk, out):
    for p in range(4):
        for r in range(4):
            taps = [w[p, q, r].astype(F32) for q in range(4)]
            wk[pl.ds((p * 4 + r) * 32, 32), :] = jnp.concatenate(taps, axis=0).astype(BF)
    out[...] = wk[...].T


def mine_body(feat_hbm, cot_hbm, w_hbm, flat, edge, rows, wt, w_out, feat, cot, fs, cs, wk, sems):
    core = core_index()
    loads = [
        pltpu.make_async_copy(feat_hbm, feat, sems.at[0]),
        pltpu.make_async_copy(cot_hbm, cot, sems.at[1]),
        pltpu.make_async_copy(w_hbm, w_out, sems.at[2]),
    ]
    for load in loads:
        load.start()
    loads[0].wait()
    tiles = cell_rows(feat, fs, range(8))
    for v in range(8):
        flat[v] = tiles[v].astype(BF)
    loads[1].wait()
    fine_rows(cot, cs)
    edge[...] = edge_rows(tiles, cs, core).astype(BF)
    half_rows(cs, core, rows)
    loads[2].wait()
    turned_weights(w_out, wk, wt)


def mine(feat, cot, w):
    return call(
        mine_body,
        (s((8, 16, 128)), s((48, 128)), s((4, 72, 128), F32), s((256, 512)), s((4, 4, 4, 8, 256))),
        [
            pltpu.VMEM((16, 2, 8, 64), BF),
            pltpu.VMEM((8, 4, 16, 128), BF),
            pltpu.VMEM((256, 64), F32),
            pltpu.VMEM((512, 128), F32),
            pltpu.VMEM((512, 256), BF),
            pltpu.SemaphoreType.DMA((3,)),
        ],
        (0, 1500000),
        in_specs=[pl.BlockSpec(memory_space=pltpu.HBM)] * 3,
    )(feat, cot, w)


def pack_body(feat, cot, flat, edge, both, out, fs, cs):
    core = core_index()
    tiles = cell_rows(feat, fs, range(8))
    for v in range(8):
        own = flat[v].astype(F32)
        both[v] = jnp.concatenate([pick(core, own, tiles[v]), pick(core, tiles[v], own)], axis=0).astype(BF)
    fine_rows(cot, cs)
    own, other = edge[...].astype(F32), edge_rows(tiles, cs, core)
    features = [pick(core, own[:16], other[:16]), pick(core, other[:16], own[:16])]
    out[...] = jnp.concatenate(features + [own[16:], other[16:]], axis=0).astype(BF)


def pack(feat, cot, flat, edge):
    return call(
        pack_body,
        (s((8, 32, 128)), s((96, 128))),
        [pltpu.VMEM((256, 64), F32), pltpu.VMEM((512, 128), F32)],
        (0, 600000),
    )(feat, cot, flat, edge)


def turn_body(cot, w, rows, wt, cs, wk):
    fine_rows(cot, cs)
    half_rows(cs, core_index(), rows)
    turned_weights(w, wk, wt)


def turn(cot, w):
    return call(
        turn_body,
        (s((4, 72, 128), F32), s((256, 512))),
        [pltpu.VMEM((512, 128), F32), pltpu.VMEM((512, 256), BF)],
        (0, 1500000),
    )(cot, w)


def merge_body(both, halo, halo_o, out):
    core = core_index()
    own, other = halo[0:32, :].astype(F32), halo_o[0:32, :].astype(F32)
    out[0] = pick(core, own, other).astype(BF)
    out[9] = pick(core, other, own).astype(BF)
    for v in range(8):
        out[v + 1] = both[v]


def merge(both, halo, halo_o):
    return call(merge_body, s((10, 32, 128)), [], (0, 200000))(both, halo, halo_o)


def grad_body(wt, wt_o, rows, rows_o, halo, out, cols):
    core = core_index()
    i = lax.broadcasted_iota(jnp.int32, (256, 512), 0)
    j = lax.broadcasted_iota(jnp.int32, (256, 512), 1)
    want = 2 * (j & 63) + (j >> 7) - 1
    same = (i >> 7) == ((j >> 6) & 1)
    select = jnp.where(((i & 127) == want) & same, 1.0, 0.0).astype(BF)
    zero = jnp.zeros((80, 128), BF)
    for k, body in enumerate((rows, rows_o)):
        plane = []
        for a in range(4):
            at = 32 + (k * 4 + a) * 8
            edge = halo[at : at + 8, :].astype(F32)
            whole = pick(
                core, jnp.concatenate([edge, body[a]], axis=0), jnp.concatenate([body[a], edge], axis=0)
            )
            plane.append(whole.astype(BF))
        for p in range(4):
            low = plane[p - 1] if p > 0 else zero
            high = plane[p + 1] if p < 3 else zero
            cols[k, p] = dot(jnp.concatenate([low, high], axis=1), select).astype(BF)
    for pair in range(2):
        sides = []
        for k in range(2):
            halves = []
            for v in (2 * pair, 2 * pair + 1):
                parts = [
                    cols[k, p, 16 * v : 16 * v + 32, r * 128 : (r + 1) * 128] for p in range(4) for r in range(4)
                ]
                halves.append(jnp.concatenate(parts, axis=0))
            sides.append(jnp.concatenate(halves, axis=1))
        out[:, pair * 256 : (pair + 1) * 256] = dot(wt[...], sides[0]) + dot(wt_o[...], sides[1])


def grad(wt, wt_o, rows, rows_o, halo):
    return call(
        grad_body,
        s((256, 512), F32),
        [pltpu.VMEM((2, 4, 80, 512), BF)],
        (500000000, 1400000),
    )(wt, wt_o, rows, rows_o, halo)


def total_body(parts, out, rows):
    for half in range(2):
        acc = parts[half]
        for chip in range(1, 8):
            acc = acc + parts[2 * chip + half]
        for k in range(4):
            v = 4 * half + k
            for u in range(2):
                rows[pl.ds(u * 8 + v, 16, stride=16), :] = acc[:, k * 128 + u * 64 : k * 128 + (u + 1) * 64]
    for ch in range(16):
        for u in range(2):
            out[ch, u] = rows[pl.ds(ch * 16 + u * 8, 8), :].astype(BF)


def total(parts):
    return call(total_body, s((16, 2, 8, 64)), [pltpu.VMEM((256, 64), F32)], (200000, 600000))(parts)


def up_body(weights, own, side, side_y, far, away, side_o, side_y_o, far_o, out, f, y, fine):
    me = lax.axis_index("chan")
    core = lax.rem(me, 2)
    x, row = lax.rem(lax.div(me, 2), 4), lax.div(me, 8)
    near = lax.rem(x + 3 + 2 * core, 4)
    near_o = lax.rem(x + 5 - 2 * core, 4)
    across = lax.rem(x + 2, 4)
    flip = 1 - row
    far_row = row + core - 2 * row * core
    places = (
        (own, x, row),
        (away, x, flip),
        (side, near, row),
        (side_o, near_o, row),
        (side_y, near, flip),
        (side_y_o, near_o, flip),
        (far, across, far_row),
        (far_o, across, 1 - far_row),
    )
    for ref, px, py in places:
        rows = pl.ds(pl.multiple_of((py * 4 + px) * 32, 32), 32)
        for t in range(10):
            f[t, rows, :] = ref[t]
    w = weights[...]
    for t in range(5):
        y[t] = dot(w, jnp.concatenate([f[2 * t], f[2 * t + 1]], axis=1))

    def tap(p, q, r, v):
        t = v + 1
        return y[t // 2, pl.ds(((p * 4 + q) * 4 + r) * 8, 8), (t % 2) * 128 : (t % 2 + 1) * 128]

    lane = lax.broadcasted_iota(jnp.int32, (8, 128), 1)
    first_half = lane < 64
    cell = lane & 63
    ii = lax.broadcasted_iota(jnp.int32, (256, 256), 0)
    jj = lax.broadcasted_iota(jnp.int32, (256, 256), 1)
    spread = jnp.where(((jj >> 7) == ((ii >> 6) & 1)) & ((jj & 127) == 2 * (ii & 63) + (ii >> 7)), 1.0, 0.0).astype(BF)
    for pb in range(2):
        blocks = {0: [], 1: []}
        for n in range(8):
            pairs = ((1, n), (3, n - 1)) if pb == 0 else ((2, n), (0, n + 1))
            got = {0: [], 1: []}
            for r in range(4):
                t = [sum(tap(p, q, r, v) for q, v in pairs) for p in range(4)]
                moved = pltpu.roll(jnp.where(first_half, t[3], t[0]), 64, 1)
                got[0].append(t[1] + jnp.where(first_half, 0.0, moved))
                got[1].append(t[2] + jnp.where(first_half, moved, 0.0))
            for pa in range(2):
                t0, t1, t2, t3 = got[pa]
                even = t1 + jnp.where(cell == 0, 0.0, pltpu.roll(t3, 1, 1))
                odd = t2 + jnp.where(cell == 63, 0.0, pltpu.roll(t0, 127, 1))
                blocks[pa].append(jnp.concatenate([even, odd], axis=1))
        for pa in range(2):
            rows = dot(jnp.concatenate(blocks[pa], axis=0).astype(BF), spread)
            for n in range(8):
                for m in range(2):
                    fine[pl.ds((2 * m + pa) * 16 + 2 * n + pb, 8, stride=64), :] = rows[
                        n * 8 : (n + 1) * 8, m * 128 : (m + 1) * 128
                    ]
    for o in range(8):
        for a in range(4):
            out[o, a] = fine[pl.ds((o * 4 + a) * 16, 16), :].astype(BF)


def upsample(weights, *blocks):
    return call(
        up_body,
        s((8, 4, 16, 128)),
        [pltpu.VMEM((10, 256, 128), BF), pltpu.VMEM((5, 512, 256), F32), pltpu.VMEM((512, 128), F32)],
        (400000000, 1100000),
    )(weights, *blocks)


def local(features, weights, cotangent):
    tiles = lax.axis_size("space")
    chans = lax.axis_size("chan")
    at = lambda ch, sp: ch * tiles + sp
    index = lambda x, row, core: (row * 4 + x % 4) * 2 + core
    swap = [(ch, ch ^ 1) for ch in range(chans)]
    cross = []
    for ch in range(chans):
        for sp in range(tiles):
            to = sp + 1 - 2 * (ch % 2)
            if 0 <= to < tiles:
                cross.append((at(ch, sp), at(ch, to)))
    chips = [(x, row, core) for row in range(2) for x in range(4) for core in range(2)]
    beside = [(index(x, row, c), index(x + 1 - 2 * c, row, c)) for x, row, c in chips]
    beside_y = [(index(x, row, c), index(x + 1 - 2 * c, 1 - row, c)) for x, row, c in chips]
    over = [(index(x, row, c), index(x + 2, (row + c) % 2, c)) for x, row, c in chips]
    over_y = [(index(x, row, c), index(x, 1 - row, c)) for x, row, c in chips]
    send = lambda a, pairs: lax.ppermute(a, "chan", pairs)

    w_own = jnp.transpose(weights, (0, 1, 2, 4, 3))
    cot_other, feat_other, w_other = send(cotangent, swap), send(features, swap), send(w_own, swap)
    flat, edge, rows, wt, w_near = mine(features, cotangent, w_own)
    cot_other, feat_other, w_other, flat = lax.optimization_barrier((cot_other, feat_other, w_other, flat))
    both, edges = pack(feat_other, cot_other, flat, edge)
    halo = lax.ppermute(edges, ("chan", "space"), cross)
    rows_other, wt_other = turn(cot_other, w_other)
    halo_other = send(halo, swap)

    partial = grad(wt, wt_other, rows, rows_other, halo)
    chip = merge(both, halo, halo_other)
    side, away = send(chip, beside), send(chip, over_y)
    pieces = lax.all_to_all(partial.reshape(16, 16, 512), "chan", 0, 0, tiled=True)
    side_y, far = send(chip, beside_y), send(chip, over)
    side_o, side_y_o, far_o = send(side, swap), send(side_y, swap), send(far, swap)
    decoded = upsample(w_near.reshape(512, 256), chip, side, side_y, far, away, side_o, side_y_o, far_o)
    return decoded, total(pieces)


def solution(mesh):
    return jax.shard_map(
        local,
        mesh=mesh,
        in_specs=(
            P("chan", None, "space", None),
            P(None, None, None, None, "chan"),
            P("chan", None, "space", None),
        ),
        out_specs=(P("chan", None, "space", None), P("chan", None, "space", None)),
        check_vma=False,
    )
```

```python
import jax
import jax.numpy as jnp
from jax import lax
from jax.experimental import pallas as pl
from jax.experimental.pallas import tpu as pltpu
from jax.sharding import PartitionSpec as P

BF = jnp.bfloat16
F32 = jnp.float32


def s(shape, kind=BF):
    return jax.ShapeDtypeStruct(shape, kind)


def call(body, outs, scratch, cost, limit=12 * 1024, **kw):
    return pl.pallas_call(
        body,
        out_shape=outs,
        scratch_shapes=scratch,
        cost_estimate=pl.CostEstimate(flops=cost[0], bytes_accessed=cost[1], transcendentals=0),
        compiler_params=pltpu.CompilerParams(vmem_limit_bytes=limit * 1024),
        **kw,
    )


def dot(a, b, dims=((1,), (0,))):
    return lax.dot_general(a, b, (dims, ((), ())), preferred_element_type=F32)


def core_index():
    return lax.rem(lax.axis_index("chan"), 2)


def pick(core, zero, one):
    return jnp.where(jnp.full(zero.shape, core, jnp.int32) == 0, zero, one)


def cell_rows(feat, fs, rows):
    for ch in range(16):
        for u in range(2):
            fs[pl.ds(ch * 16 + u * 8, 8), :] = feat[ch, u].astype(F32)
    return {
        v: jnp.concatenate([fs[pl.ds(v, 16, stride=16), :], fs[pl.ds(8 + v, 16, stride=16), :]], axis=1)
        for v in rows
    }


def fine_rows(cot, cs):
    for o in range(8):
        for a in range(4):
            cs[pl.ds((o * 4 + a) * 16, 16), :] = cot[o, a].astype(F32)


def turned_rows(cs, out):
    for a in range(4):
        for n in range(16):
            out[a, n * 8 : (n + 1) * 8, :] = cs[pl.ds(a * 16 + n, 8, stride=64), :]


def edge_rows(tiles, cs, core):
    first = jnp.concatenate([tiles[0]] + [cs[pl.ds(a * 16, 8, stride=64), :] for a in range(4)], axis=0)
    last = jnp.concatenate([tiles[7]] + [cs[pl.ds(a * 16 + 15, 8, stride=64), :] for a in range(4)], axis=0)
    return pick(core, last, first)


def turned_weights(w, wk, out):
    for p in range(4):
        for r in range(4):
            taps = [w[p, q, r].astype(F32) for q in range(4)]
            wk[pl.ds((p * 4 + r) * 32, 32), :] = jnp.concatenate(taps, axis=0).astype(BF)
    out[...] = wk[...].T


def mine_body(feat_hbm, cot_hbm, flat, edge, cot, feat, fs, cs, sems):
    core = core_index()
    loads = [pltpu.make_async_copy(feat_hbm, feat, sems.at[0]), pltpu.make_async_copy(cot_hbm, cot, sems.at[1])]
    for load in loads:
        load.start()
    loads[0].wait()
    tiles = cell_rows(feat, fs, range(8))
    for v in range(8):
        flat[v] = tiles[v].astype(BF)
    loads[1].wait()
    fine_rows(cot, cs)
    edge[...] = edge_rows(tiles, cs, core).astype(BF)


def mine(feat, cot):
    return call(
        mine_body,
        (s((8, 16, 128)), s((48, 128)), s((8, 4, 16, 128))),
        [
            pltpu.VMEM((16, 2, 8, 64), BF),
            pltpu.VMEM((256, 64), F32),
            pltpu.VMEM((512, 128), F32),
            pltpu.SemaphoreType.DMA((2,)),
        ],
        (0, 1000000),
        in_specs=[pl.BlockSpec(memory_space=pltpu.HBM)] * 2,
    )(*(pltpu.with_memory_space_constraint(a, pltpu.HBM) for a in (feat, cot)))


def pack_body(feat, cot, flat, edge, both, out, fs, cs):
    core = core_index()
    tiles = cell_rows(feat, fs, range(8))
    for v in range(8):
        own = flat[v].astype(F32)
        both[v] = jnp.concatenate([pick(core, own, tiles[v]), pick(core, tiles[v], own)], axis=0).astype(BF)
    fine_rows(cot, cs)
    own, other = edge[...].astype(F32), edge_rows(tiles, cs, core)
    features = [pick(core, own[:16], other[:16]), pick(core, other[:16], own[:16])]
    out[...] = jnp.concatenate(features + [own[16:], other[16:]], axis=0).astype(BF)


def pack(feat, cot, flat, edge):
    return call(
        pack_body,
        (s((8, 32, 128)), s((96, 128))),
        [pltpu.VMEM((256, 64), F32), pltpu.VMEM((512, 128), F32)],
        (0, 600000),
    )(feat, cot, flat, edge)


def turn_body(cot, cot_o, w_o, w_hbm, rows, wt, w, cs, wk, sem):
    load = pltpu.make_async_copy(w_hbm, w, sem)
    load.start()
    for k, x in enumerate((cot, cot_o)):
        fine_rows(x, cs)
        turned_rows(cs, rows.at[k])
    turned_weights(w_o, wk, wt.at[1])
    load.wait()
    turned_weights(w, wk, wt.at[0])


def turn(cot, cot_o, w_o, w):
    return call(
        turn_body,
        (s((2, 4, 128, 128), F32), s((2, 256, 512)), s((4, 4, 4, 8, 256))),
        [pltpu.VMEM((512, 128), F32), pltpu.VMEM((512, 256), BF), pltpu.SemaphoreType.DMA],
        (0, 1500000),
        in_specs=[pl.BlockSpec(memory_space=pltpu.VMEM)] * 3 + [pl.BlockSpec(memory_space=pltpu.HBM)],
    )(cot, cot_o, w_o, pltpu.with_memory_space_constraint(w, pltpu.HBM))


def place():
    me = lax.axis_index("chan")
    core = lax.rem(me, 2)
    return lax.rem(lax.div(me, 2), 4), lax.div(me, 8), core


def either(core, zero, one):
    return zero + core * (one - zero)


def grad_body(wt, rows, halo, halo_o, both, far, side_y, side, away, kept, cols, chosen):
    x, row, core = place()
    chip = lambda px, py: pl.multiple_of((py * 4 + px) * 32, 32)
    near = lax.rem(x + 1 + 2 * core, 4)
    starts = (
        chip(lax.rem(x + 2, 4), either(core, row, 1 - row)),
        chip(near, 1 - row),
        chip(near, row),
    )
    for k in range(2):
        for n, start in enumerate(starts):
            chosen[k, n * 32 : (n + 1) * 32, :] = wt[k, pl.ds(start, 32), :]
        for n, py in ((6, 1 - row), (7, row)):
            start = pl.multiple_of(chip(x, py) + core * 16, 16)
            chosen[k, n * 16 : (n + 1) * 16, :] = wt[k, pl.ds(start, 16), :]

    top = [pick(core, halo[...].astype(F32), halo_o[...].astype(F32))]
    low = [pick(core, halo_o[...].astype(F32), halo[...].astype(F32))]
    for out in (far, side_y, side, away):
        out[0] = top[0][:32].astype(BF)
        out[9] = low[0][:32].astype(BF)
        for v in range(8):
            out[v + 1] = both[v]

    i = lax.broadcasted_iota(jnp.int32, (256, 512), 0)
    j = lax.broadcasted_iota(jnp.int32, (256, 512), 1)
    want = 2 * (j & 63) + (j >> 7) - 1
    same = (i >> 7) == ((j >> 6) & 1)
    select = jnp.where(((i & 127) == want) & same, 1.0, 0.0).astype(BF)
    zero = jnp.zeros((144, 128), BF)
    for k in range(2):
        plane = []
        for a in range(4):
            mine_at, theirs_at = 32 + (k * 4 + a) * 8, 32 + ((1 - k) * 4 + a) * 8
            own, other = halo[mine_at : mine_at + 8, :].astype(F32), halo_o[theirs_at : theirs_at + 8, :].astype(F32)
            whole = jnp.concatenate([pick(core, own, other), rows[k, a], pick(core, other, own)], axis=0)
            plane.append(whole.astype(BF))
        for p in range(4):
            before = plane[p - 1] if p > 0 else zero
            after = plane[p + 1] if p < 3 else zero
            cols[k, p] = dot(jnp.concatenate([before, after], axis=1), select).astype(BF)
    for pair in range(4):
        total = None
        for k in range(2):
            halves = []
            for v in (2 * pair, 2 * pair + 1):
                parts = [
                    cols[k, p, 16 * v : 16 * v + 32, r * 128 : (r + 1) * 128] for p in range(4) for r in range(4)
                ]
                halves.append(jnp.concatenate(parts, axis=0))
            part = dot(chosen[k], jnp.concatenate(halves, axis=1))
            total = part if total is None else total + part
        high = total.astype(BF)
        rest = (total - high.astype(F32)).astype(BF)
        for half in range(2):
            v, lanes = 2 * pair + half, slice(half * 128, (half + 1) * 128)
            for n, out in enumerate((far, side_y, side)):
                out[10 + v] = high[n * 32 : (n + 1) * 32, lanes]
                out[18 + v] = rest[n * 32 : (n + 1) * 32, lanes]
            away[10 + v, 0:16, :] = high[96:112, lanes]
            away[10 + v, 16:32, :] = rest[96:112, lanes]
            kept[v] = total[112:128, lanes]


def grad(wt, rows, halo, halo_o, both):
    whole = s((26, 32, 128))
    return call(
        grad_body,
        (whole, whole, whole, s((18, 32, 128)), s((8, 16, 128), F32)),
        [pltpu.VMEM((2, 4, 144, 512), BF), pltpu.VMEM((2, 128, 512), BF)],
        (500000000, 2500000),
    )(wt, rows, halo, halo_o, both)


def total_body(kept, away, *refs):
    arrived, (out, rows) = refs[:6], refs[6:]
    mine = pl.ds(pl.multiple_of(core_index() * 16, 16), 16)
    for v in range(8):
        acc = kept[v] + (away[10 + v, 0:16, :].astype(F32) + away[10 + v, 16:32, :].astype(F32))
        for ref in arrived:
            acc = acc + (ref[10 + v, mine, :].astype(F32) + ref[18 + v, mine, :].astype(F32))
        for u in range(2):
            rows[pl.ds(u * 8 + v, 16, stride=16), :] = acc[:, u * 64 : (u + 1) * 64]
    for ch in range(16):
        for u in range(2):
            out[ch, u] = rows[pl.ds(ch * 16 + u * 8, 8), :].astype(BF)


def total(kept, away, *arrived):
    return call(total_body, s((16, 2, 8, 64)), [pltpu.VMEM((256, 64), F32)], (200000, 600000))(kept, away, *arrived)


def up_body(weights, own, side, side_y, far, away, side_o, side_y_o, far_o, out, f, y, fine):
    x, row, core = place()
    near = lax.rem(x + 3 + 2 * core, 4)
    near_o = lax.rem(x + 5 - 2 * core, 4)
    across = lax.rem(x + 2, 4)
    flip = 1 - row
    far_row = either(core, row, flip)
    places = (
        (own, x, row),
        (away, x, flip),
        (side, near, row),
        (side_o, near_o, row),
        (side_y, near, flip),
        (side_y_o, near_o, flip),
        (far, across, far_row),
        (far_o, across, 1 - far_row),
    )
    for ref, px, py in places:
        rows = pl.ds(pl.multiple_of((py * 4 + px) * 32, 32), 32)
        for t in range(10):
            f[t, rows, :] = ref[t]
    w = weights[...]
    for t in range(5):
        y[t] = dot(w, jnp.concatenate([f[2 * t], f[2 * t + 1]], axis=1))

    def tap(p, q, r, v):
        t = v + 1
        return y[t // 2, pl.ds(((p * 4 + q) * 4 + r) * 8, 8), (t % 2) * 128 : (t % 2 + 1) * 128]

    lane = lax.broadcasted_iota(jnp.int32, (8, 128), 1)
    first_half = lane < 64
    cell = lane & 63
    ii = lax.broadcasted_iota(jnp.int32, (256, 256), 0)
    jj = lax.broadcasted_iota(jnp.int32, (256, 256), 1)
    spread = jnp.where(((jj >> 7) == ((ii >> 6) & 1)) & ((jj & 127) == 2 * (ii & 63) + (ii >> 7)), 1.0, 0.0).astype(BF)
    for pb in range(2):
        blocks = {0: [], 1: []}
        for n in range(8):
            pairs = ((1, n), (3, n - 1)) if pb == 0 else ((2, n), (0, n + 1))
            got = {0: [], 1: []}
            for r in range(4):
                t = [sum(tap(p, q, r, v) for q, v in pairs) for p in range(4)]
                moved = pltpu.roll(jnp.where(first_half, t[3], t[0]), 64, 1)
                got[0].append(t[1] + jnp.where(first_half, 0.0, moved))
                got[1].append(t[2] + jnp.where(first_half, moved, 0.0))
            for pa in range(2):
                t0, t1, t2, t3 = got[pa]
                even = t1 + jnp.where(cell == 0, 0.0, pltpu.roll(t3, 1, 1))
                odd = t2 + jnp.where(cell == 63, 0.0, pltpu.roll(t0, 127, 1))
                blocks[pa].append(jnp.concatenate([even, odd], axis=1))
        for pa in range(2):
            rows = dot(jnp.concatenate(blocks[pa], axis=0).astype(BF), spread)
            for n in range(8):
                for m in range(2):
                    fine[pl.ds((2 * m + pa) * 16 + 2 * n + pb, 8, stride=64), :] = rows[
                        n * 8 : (n + 1) * 8, m * 128 : (m + 1) * 128
                    ]
    for o in range(8):
        for a in range(4):
            out[o, a] = fine[pl.ds((o * 4 + a) * 16, 16), :].astype(BF)


def upsample(weights, *blocks):
    return call(
        up_body,
        s((8, 4, 16, 128)),
        [pltpu.VMEM((10, 256, 128), BF), pltpu.VMEM((5, 512, 256), F32), pltpu.VMEM((512, 128), F32)],
        (400000000, 1100000),
    )(weights, *blocks)


def local(features, weights, cotangent):
    tiles = lax.axis_size("space")
    chans = lax.axis_size("chan")
    at = lambda ch, sp: ch * tiles + sp
    index = lambda x, row, core: (row * 4 + x % 4) * 2 + core
    swap = [(ch, ch ^ 1) for ch in range(chans)]
    cross = []
    for ch in range(chans):
        for sp in range(tiles):
            to = sp + 1 - 2 * (ch % 2)
            if 0 <= to < tiles:
                cross.append((at(ch, sp), at(ch, to)))
    chips = [(x, row, core) for row in range(2) for x in range(4) for core in range(2)]
    beside = [(index(x, row, c), index(x + 1 - 2 * c, row, c)) for x, row, c in chips]
    beside_y = [(index(x, row, c), index(x + 1 - 2 * c, 1 - row, c)) for x, row, c in chips]
    over = [(index(x, row, c), index(x + 2, (row + c) % 2, c)) for x, row, c in chips]
    over_y = [(index(x, row, c), index(x, 1 - row, c)) for x, row, c in chips]
    send = lambda a, pairs: lax.ppermute(a, "chan", pairs)

    w_own = jnp.transpose(weights, (0, 1, 2, 4, 3))
    cot_other, feat_other, w_other = send(cotangent, swap), send(features, swap), send(w_own, swap)
    flat, edge, cot = mine(features, cotangent)
    cot_other, feat_other, w_other, flat = lax.optimization_barrier((cot_other, feat_other, w_other, flat))
    both, edges = pack(feat_other, cot_other, flat, edge)
    halo = lax.ppermute(edges, ("chan", "space"), cross)
    halo_other = send(halo, swap)
    rows, wt, w_near = turn(cot, cot_other, w_other, w_own)
    far, side_y, side, away, kept = grad(wt, rows, halo, halo_other, both)
    own = away

    far, side_y = send(far, over), send(side_y, beside_y)
    side, away = send(side, beside), send(away, over_y)
    far_o, side_y_o, side_o = send(far, swap), send(side_y, swap), send(side, swap)
    decoded = upsample(w_near.reshape(512, 256), own, side, side_y, far, away, side_o, side_y_o, far_o)
    return decoded, total(kept, away, side, side_y, far, side_o, side_y_o, far_o)


def solution(mesh):
    return jax.shard_map(
        local,
        mesh=mesh,
        in_specs=(
            P("chan", None, "space", None),
            P(None, None, None, None, "chan"),
            P("chan", None, "space", None),
        ),
        out_specs=(P("chan", None, "space", None), P("chan", None, "space", None)),
        check_vma=False,
    )
```

```python
import jax
import jax.numpy as jnp
from jax import lax
from jax.experimental import pallas as pl
from jax.experimental.pallas import tpu as pltpu
from jax.sharding import PartitionSpec as P

BF = jnp.bfloat16
F32 = jnp.float32


def s(shape, kind=BF):
    return jax.ShapeDtypeStruct(shape, kind)


def call(body, outs, scratch, cost, limit=12 * 1024, **kw):
    return pl.pallas_call(
        body,
        out_shape=outs,
        scratch_shapes=scratch,
        cost_estimate=pl.CostEstimate(flops=cost[0], bytes_accessed=cost[1], transcendentals=0),
        compiler_params=pltpu.CompilerParams(vmem_limit_bytes=limit * 1024),
        **kw,
    )


def dot(a, b, dims=((1,), (0,))):
    return lax.dot_general(a, b, (dims, ((), ())), preferred_element_type=F32)


def core_index():
    return lax.rem(lax.axis_index("chan"), 2)


def pick(core, zero, one):
    return jnp.where(jnp.full(zero.shape, core, jnp.int32) == 0, zero, one)


def cell_rows(feat, fs, rows):
    for ch in range(16):
        for u in range(2):
            fs[pl.ds(ch * 16 + u * 8, 8), :] = feat[ch, u].astype(F32)
    return [
        jnp.concatenate([fs[pl.ds(v, 16, stride=16), :], fs[pl.ds(8 + v, 16, stride=16), :]], axis=1)
        for v in rows
    ]


def fine_rows(cot, cs):
    for o in range(8):
        for a in range(4):
            cs[pl.ds((o * 4 + a) * 16, 16), :] = cot[o, a].astype(F32)


def edge_rows(feat, cot, fs, cs):
    core = core_index()
    first, last = cell_rows(feat, fs, (0, 7))
    fine_rows(cot, cs)
    turned = [
        pick(core, cs[pl.ds(a * 16 + 15, 8, stride=64), :], cs[pl.ds(a * 16, 8, stride=64), :]) for a in range(4)
    ]
    return pick(core, last, first), turned


def turned_weights(w, wk, out):
    for p in range(4):
        for r in range(4):
            taps = [w[p, q, r].astype(F32) for q in range(4)]
            wk[pl.ds((p * 4 + r) * 32, 32), :] = jnp.concatenate(taps, axis=0).astype(BF)
    out[...] = wk[...].T


def selection():
    i = lax.broadcasted_iota(jnp.int32, (256, 512), 0)
    j = lax.broadcasted_iota(jnp.int32, (256, 512), 1)
    want = 2 * (j & 63) + (j >> 7) - 1
    same = (i >> 7) == ((j >> 6) & 1)
    return jnp.where(((i & 127) == want) & same, 1.0, 0.0).astype(BF)


def spreading():
    i = lax.broadcasted_iota(jnp.int32, (256, 256), 0)
    j = lax.broadcasted_iota(jnp.int32, (256, 256), 1)
    return jnp.where(((j >> 7) == ((i >> 6) & 1)) & ((j & 127) == 2 * (i & 63) + (i >> 7)), 1.0, 0.0).astype(BF)


def mine_body(feat_hbm, cot_hbm, edge, feat, cot, select, spread, fs, cs, sems):
    loads = [pltpu.make_async_copy(feat_hbm, feat, sems.at[0]), pltpu.make_async_copy(cot_hbm, cot, sems.at[1])]
    for load in loads:
        load.start()
    select[...] = selection()
    spread[...] = spreading()
    for load in loads:
        load.wait()
    row, turned = edge_rows(feat, cot, fs, cs)
    edge[...] = jnp.concatenate([row] + turned, axis=0)


def mine(feat, cot):
    return call(
        mine_body,
        (s((48, 128), F32), s((16, 2, 8, 64)), s((8, 4, 16, 128)), s((256, 512)), s((256, 256))),
        [pltpu.VMEM((256, 64), F32), pltpu.VMEM((512, 128), F32), pltpu.SemaphoreType.DMA((2,))],
        (0, 1000000),
        in_specs=[pl.BlockSpec(memory_space=pltpu.HBM)] * 2,
    )(*(pltpu.with_memory_space_constraint(a, pltpu.HBM) for a in (feat, cot)))


def pack_body(feat, cot, edge, out, fs, cs):
    core = core_index()
    row, turned = edge_rows(feat, cot, fs, cs)
    own = edge[0:16, :]
    out[...] = jnp.concatenate([pick(core, own, row), pick(core, row, own), edge[16:48, :]] + turned, axis=0).astype(BF)


def pack(feat, cot, edge):
    return call(
        pack_body,
        s((96, 128)),
        [pltpu.VMEM((256, 64), F32), pltpu.VMEM((512, 128), F32)],
        (0, 600000),
    )(feat, cot, edge)


def place():
    me = lax.axis_index("chan")
    core = lax.rem(me, 2)
    return lax.rem(lax.div(me, 2), 4), lax.div(me, 8), core


def either(core, zero, one):
    return zero + core * (one - zero)


def columns(planes, p, select):
    zero = jnp.zeros_like(planes[0])
    before = planes[p - 1] if p > 0 else zero
    after = planes[p + 1] if p < 3 else zero
    return dot(jnp.concatenate([before, after], axis=1), select).astype(BF)


def ready_body(feat, feat_o, cot, cot_o, w_o, select_ref, w_hbm, both, chosen, cols, ends, w, fs, cs, wk, wt, sem):
    load = pltpu.make_async_copy(w_hbm, w, sem)
    load.start()
    x, row, core = place()
    own, other = cell_rows(feat, fs, range(8)), cell_rows(feat_o, fs, range(8))
    for v in range(8):
        both[v] = jnp.concatenate([pick(core, own[v], other[v]), pick(core, other[v], own[v])], axis=0).astype(BF)
    select = select_ref[...]
    empty = jnp.zeros((8, 128), F32)
    for k, ref in enumerate((cot, cot_o)):
        fine_rows(ref, cs)
        planes = []
        for a in range(4):
            rows = [cs[pl.ds(a * 16 + n, 8, stride=64), :] for n in range(16)]
            ends[k, a, 0:8, :], ends[k, a, 8:16, :] = rows[0], rows[15]
            planes.append(jnp.concatenate([empty] + rows + [empty], axis=0).astype(BF))
        for p in range(4):
            cols[k, p] = columns(planes, p, select)
    chip = lambda px, py: pl.multiple_of((py * 4 + px) * 32, 32)
    near = lax.rem(x + 1 + 2 * core, 4)
    starts = (
        chip(lax.rem(x + 2, 4), either(core, row, 1 - row)),
        chip(near, 1 - row),
        chip(near, row),
    )
    for k, ref in ((1, w_o), (0, w)):
        if k == 0:
            load.wait()
        turned_weights(ref, wk, wt)
        for n, start in enumerate(starts):
            chosen[k, n * 32 : (n + 1) * 32, :] = wt[pl.ds(start, 32), :]
        for n, py in ((6, 1 - row), (7, row)):
            start = pl.multiple_of(chip(x, py) + core * 16, 16)
            chosen[k, n * 16 : (n + 1) * 16, :] = wt[pl.ds(start, 16), :]


def ready(feat, feat_o, cot, cot_o, w_o, select, w):
    return call(
        ready_body,
        (
            s((8, 32, 128)),
            s((2, 128, 512)),
            s((2, 4, 144, 512)),
            s((2, 4, 16, 128), F32),
            s((4, 4, 4, 8, 256)),
        ),
        [
            pltpu.VMEM((256, 64), F32),
            pltpu.VMEM((512, 128), F32),
            pltpu.VMEM((512, 256), BF),
            pltpu.VMEM((256, 512), BF),
            pltpu.SemaphoreType.DMA,
        ],
        (200000000, 2500000),
        in_specs=[pl.BlockSpec(memory_space=pltpu.VMEM)] * 6 + [pl.BlockSpec(memory_space=pltpu.HBM)],
    )(feat, feat_o, cot, cot_o, w_o, select, pltpu.with_memory_space_constraint(w, pltpu.HBM))


def grad_body(chosen, cols, ends, select_ref, halo, halo_o, both, far, side_y, side, away, kept):
    core = core_index()
    up = pick(core, halo[0:32, :].astype(F32), halo_o[0:32, :].astype(F32)).astype(BF)
    down = pick(core, halo_o[0:32, :].astype(F32), halo[0:32, :].astype(F32)).astype(BF)
    for out in (far, side_y, side, away):
        out[0], out[9] = up, down
        for v in range(8):
            out[v + 1] = both[v]
    select = select_ref[...]
    tips = {}
    for k in range(2):
        planes = []
        for a in range(4):
            mine_at, theirs_at = 32 + (k * 4 + a) * 8, 32 + ((1 - k) * 4 + a) * 8
            own, other = halo[mine_at : mine_at + 8, :].astype(F32), halo_o[theirs_at : theirs_at + 8, :].astype(F32)
            pieces = [pick(core, own, other), ends[k, a], pick(core, other, own)]
            planes.append(jnp.concatenate(pieces, axis=0).astype(BF))
        for p in range(4):
            tips[k, p] = columns(planes, p, select)
    for pair in range(4):
        total = None
        for k in range(2):
            halves = []
            for v in (2 * pair, 2 * pair + 1):
                parts = []
                for p in range(4):
                    for r in range(4):
                        lanes = slice(r * 128, (r + 1) * 128)
                        if v == 0:
                            parts += [tips[k, p][0:16, lanes], cols[k, p, 16:32, lanes]]
                        elif v == 7:
                            parts += [cols[k, p, 112:128, lanes], tips[k, p][16:32, lanes]]
                        else:
                            parts.append(cols[k, p, 16 * v : 16 * v + 32, lanes])
                halves.append(jnp.concatenate(parts, axis=0))
            part = dot(chosen[k], jnp.concatenate(halves, axis=1))
            total = part if total is None else total + part
        high = total.astype(BF)
        rest = (total - high.astype(F32)).astype(BF)
        for half in range(2):
            v, lanes = 2 * pair + half, slice(half * 128, (half + 1) * 128)
            for n, out in enumerate((far, side_y, side)):
                out[10 + v] = high[n * 32 : (n + 1) * 32, lanes]
                out[18 + v] = rest[n * 32 : (n + 1) * 32, lanes]
            away[10 + v, 0:16, :] = high[96:112, lanes]
            away[10 + v, 16:32, :] = rest[96:112, lanes]
            kept[v] = total[112:128, lanes]


def grad(*args):
    whole = s((26, 32, 128))
    return call(
        grad_body,
        (whole, whole, whole, s((18, 32, 128)), s((8, 16, 128), F32)),
        [],
        (400000000, 2500000),
    )(*args)


def total_body(kept, away, *refs):
    arrived, (out, rows) = refs[:6], refs[6:]
    mine = pl.ds(pl.multiple_of(core_index() * 16, 16), 16)
    for v in range(8):
        acc = kept[v] + (away[10 + v, 0:16, :].astype(F32) + away[10 + v, 16:32, :].astype(F32))
        for ref in arrived:
            acc = acc + (ref[10 + v, mine, :].astype(F32) + ref[18 + v, mine, :].astype(F32))
        for u in range(2):
            rows[pl.ds(u * 8 + v, 16, stride=16), :] = acc[:, u * 64 : (u + 1) * 64]
    for ch in range(16):
        for u in range(2):
            out[ch, u] = rows[pl.ds(ch * 16 + u * 8, 8), :].astype(BF)


def up_body(weights, spread_ref, own, side, side_y, far, away, side_o, side_y_o, far_o, out, f, y, fine):
    x, row, core = place()
    near = lax.rem(x + 3 + 2 * core, 4)
    near_o = lax.rem(x + 5 - 2 * core, 4)
    across = lax.rem(x + 2, 4)
    flip = 1 - row
    far_row = either(core, row, flip)
    places = (
        (own, x, row),
        (away, x, flip),
        (side, near, row),
        (side_o, near_o, row),
        (side_y, near, flip),
        (side_y_o, near_o, flip),
        (far, across, far_row),
        (far_o, across, 1 - far_row),
    )
    for ref, px, py in places:
        rows = pl.ds(pl.multiple_of((py * 4 + px) * 32, 32), 32)
        for t in range(10):
            f[t, rows, :] = ref[t]
    w = weights[...]
    for t in range(5):
        y[t] = dot(w, jnp.concatenate([f[2 * t], f[2 * t + 1]], axis=1))

    def tap(p, q, r, v):
        t = v + 1
        return y[t // 2, pl.ds(((p * 4 + q) * 4 + r) * 8, 8), (t % 2) * 128 : (t % 2 + 1) * 128]

    lane = lax.broadcasted_iota(jnp.int32, (8, 128), 1)
    first_half = lane < 64
    cell = lane & 63
    spread = spread_ref[...]
    for pb in range(2):
        blocks = {0: [], 1: []}
        for n in range(8):
            pairs = ((1, n), (3, n - 1)) if pb == 0 else ((2, n), (0, n + 1))
            got = {0: [], 1: []}
            for r in range(4):
                t = [sum(tap(p, q, r, v) for q, v in pairs) for p in range(4)]
                moved = pltpu.roll(jnp.where(first_half, t[3], t[0]), 64, 1)
                got[0].append(t[1] + jnp.where(first_half, 0.0, moved))
                got[1].append(t[2] + jnp.where(first_half, moved, 0.0))
            for pa in range(2):
                t0, t1, t2, t3 = got[pa]
                even = t1 + jnp.where(cell == 0, 0.0, pltpu.roll(t3, 1, 1))
                odd = t2 + jnp.where(cell == 63, 0.0, pltpu.roll(t0, 127, 1))
                blocks[pa].append(jnp.concatenate([even, odd], axis=1))
        for pa in range(2):
            rows = dot(jnp.concatenate(blocks[pa], axis=0).astype(BF), spread)
            for n in range(8):
                for m in range(2):
                    fine[pl.ds((2 * m + pa) * 16 + 2 * n + pb, 8, stride=64), :] = rows[
                        n * 8 : (n + 1) * 8, m * 128 : (m + 1) * 128
                    ]
    for o in range(8):
        for a in range(4):
            out[o, a] = fine[pl.ds((o * 4 + a) * 16, 16), :].astype(BF)


def last_body(weights, spread, own, kept, side, side_y, far, away, side_o, side_y_o, far_o, up, grad_out, f, y, fine, rows):
    total_body(kept, away, side, side_y, far, side_o, side_y_o, far_o, grad_out, rows)
    up_body(weights, spread, own, side, side_y, far, away, side_o, side_y_o, far_o, up, f, y, fine)


def last(*args):
    return call(
        last_body,
        (s((8, 4, 16, 128)), s((16, 2, 8, 64))),
        [
            pltpu.VMEM((10, 256, 128), BF),
            pltpu.VMEM((5, 512, 256), F32),
            pltpu.VMEM((512, 128), F32),
            pltpu.VMEM((256, 64), F32),
        ],
        (400000000, 2500000),
    )(*args)


def local(features, weights, cotangent):
    tiles = lax.axis_size("space")
    chans = lax.axis_size("chan")
    at = lambda ch, sp: ch * tiles + sp
    index = lambda x, row, core: (row * 4 + x % 4) * 2 + core
    swap = [(ch, ch ^ 1) for ch in range(chans)]
    cross = []
    for ch in range(chans):
        for sp in range(tiles):
            to = sp + 1 - 2 * (ch % 2)
            if 0 <= to < tiles:
                cross.append((at(ch, sp), at(ch, to)))
    chips = [(x, row, core) for row in range(2) for x in range(4) for core in range(2)]
    beside = [(index(x, row, c), index(x + 1 - 2 * c, row, c)) for x, row, c in chips]
    beside_y = [(index(x, row, c), index(x + 1 - 2 * c, 1 - row, c)) for x, row, c in chips]
    over = [(index(x, row, c), index(x + 2, (row + c) % 2, c)) for x, row, c in chips]
    over_y = [(index(x, row, c), index(x, 1 - row, c)) for x, row, c in chips]
    send = lambda a, pairs: lax.ppermute(a, "chan", pairs)

    w_own = jnp.transpose(weights, (0, 1, 2, 4, 3))
    cot_other = send(cotangent, swap)
    feat_other = send(features, swap)
    w_other = send(w_own, swap)
    edge, feat, cot, select, spread = mine(features, cotangent)
    cot_other, feat_other, edge = lax.optimization_barrier((cot_other, feat_other, edge))
    edges = pack(feat_other, cot_other, edge)
    halo = lax.ppermute(edges, ("chan", "space"), cross)
    both, chosen, cols, ends, w_near = ready(feat, feat_other, cot, cot_other, w_other, select, w_own)
    halo_other = send(halo, swap)
    far, side_y, side, away, kept = grad(chosen, cols, ends, select, halo, halo_other, both)
    own = away

    far, side_y = send(far, over), send(side_y, beside_y)
    side, away = send(side, beside), send(away, over_y)
    far_o, side_y_o, side_o = send(far, swap), send(side_y, swap), send(side, swap)
    return last(w_near.reshape(512, 256), spread, own, kept, side, side_y, far, away, side_o, side_y_o, far_o)


def solution(mesh):
    return jax.shard_map(
        local,
        mesh=mesh,
        in_specs=(
            P("chan", None, "space", None),
            P(None, None, None, None, "chan"),
            P("chan", None, "space", None),
        ),
        out_specs=(P("chan", None, "space", None), P("chan", None, "space", None)),
        check_vma=False,
    )
```

```python
import jax
import jax.numpy as jnp
from jax import lax
from jax.experimental import pallas as pl
from jax.experimental.pallas import tpu as pltpu
from jax.sharding import PartitionSpec as P

BF = jnp.bfloat16
F32 = jnp.float32


def s(shape, kind=BF):
    return jax.ShapeDtypeStruct(shape, kind)


def call(body, outs, scratch, cost, limit=12 * 1024, **kw):
    return pl.pallas_call(
        body,
        out_shape=outs,
        scratch_shapes=scratch,
        cost_estimate=pl.CostEstimate(flops=cost[0], bytes_accessed=cost[1], transcendentals=0),
        compiler_params=pltpu.CompilerParams(vmem_limit_bytes=limit * 1024),
        **kw,
    )


def dot(a, b, dims=((1,), (0,))):
    return lax.dot_general(a, b, (dims, ((), ())), preferred_element_type=F32)


def core_index():
    return lax.rem(lax.axis_index("chan"), 2)


def pick(core, zero, one):
    return jnp.where(jnp.full(zero.shape, core, jnp.int32) == 0, zero, one)


def cell_rows(feat, fs, rows):
    for ch in range(16):
        for u in range(2):
            fs[pl.ds(ch * 16 + u * 8, 8), :] = feat[ch, u].astype(F32)
    return [
        jnp.concatenate([fs[pl.ds(v, 16, stride=16), :], fs[pl.ds(8 + v, 16, stride=16), :]], axis=1)
        for v in rows
    ]


def fine_rows(cot, cs):
    for o in range(8):
        for a in range(4):
            cs[pl.ds((o * 4 + a) * 16, 16), :] = cot[o, a].astype(F32)


def edge_rows(feat, cot, fs, cs):
    core = core_index()
    first, last = cell_rows(feat, fs, (0, 7))
    fine_rows(cot, cs)
    turned = [
        pick(core, cs[pl.ds(a * 16 + 15, 8, stride=64), :], cs[pl.ds(a * 16, 8, stride=64), :]) for a in range(4)
    ]
    return pick(core, last, first), turned


def turned_weights(w, wk, out):
    for p in range(4):
        for r in range(4):
            taps = [w[p, q, r].astype(F32) for q in range(4)]
            wk[pl.ds((p * 4 + r) * 32, 32), :] = jnp.concatenate(taps, axis=0).astype(BF)
    out[...] = wk[...].T


def selection():
    i = lax.broadcasted_iota(jnp.int32, (256, 512), 0)
    j = lax.broadcasted_iota(jnp.int32, (256, 512), 1)
    want = 2 * (j & 63) + (j >> 7) - 1
    same = (i >> 7) == ((j >> 6) & 1)
    return jnp.where(((i & 127) == want) & same, 1.0, 0.0).astype(BF)


def spreading():
    i = lax.broadcasted_iota(jnp.int32, (256, 256), 0)
    j = lax.broadcasted_iota(jnp.int32, (256, 256), 1)
    return jnp.where(((j >> 7) == ((i >> 6) & 1)) & ((j & 127) == 2 * (i & 63) + (i >> 7)), 1.0, 0.0).astype(BF)


def mine_body(feat_hbm, cot_hbm, edge, feat, cot, select, spread, fs, cs, sems):
    loads = [pltpu.make_async_copy(feat_hbm, feat, sems.at[0]), pltpu.make_async_copy(cot_hbm, cot, sems.at[1])]
    for load in loads:
        load.start()
    select[...] = selection()
    spread[...] = spreading()
    for load in loads:
        load.wait()
    row, turned = edge_rows(feat, cot, fs, cs)
    edge[...] = jnp.concatenate([row] + turned, axis=0)


def mine(feat, cot):
    return call(
        mine_body,
        (s((48, 128), F32), s((16, 2, 8, 64)), s((8, 4, 16, 128)), s((256, 512)), s((256, 256))),
        [pltpu.VMEM((256, 64), F32), pltpu.VMEM((512, 128), F32), pltpu.SemaphoreType.DMA((2,))],
        (0, 1000000),
        in_specs=[pl.BlockSpec(memory_space=pltpu.HBM)] * 2,
    )(*(pltpu.with_memory_space_constraint(a, pltpu.HBM) for a in (feat, cot)))


def pack_body(feat, cot, edge, out, fs, cs):
    core = core_index()
    row, turned = edge_rows(feat, cot, fs, cs)
    own = edge[0:16, :]
    out[...] = jnp.concatenate([pick(core, own, row), pick(core, row, own), edge[16:48, :]] + turned, axis=0).astype(BF)


def pack(feat, cot, edge):
    return call(
        pack_body,
        s((96, 128)),
        [pltpu.VMEM((256, 64), F32), pltpu.VMEM((512, 128), F32)],
        (0, 600000),
    )(feat, cot, edge)


def place():
    me = lax.axis_index("chan")
    core = lax.rem(me, 2)
    return lax.rem(lax.div(me, 2), 4), lax.div(me, 8), core


def either(core, zero, one):
    return zero + core * (one - zero)


def columns(planes, p, select):
    zero = jnp.zeros_like(planes[0])
    before = planes[p - 1] if p > 0 else zero
    after = planes[p + 1] if p < 3 else zero
    return dot(jnp.concatenate([before, after], axis=1), select).astype(BF)


def ready_body(feat, feat_o, cot, cot_o, w_o, select_ref, w_hbm, both, chosen, cols, ends, w, fs, cs, wk, wt, sem):
    load = pltpu.make_async_copy(w_hbm, w, sem)
    load.start()
    x, row, core = place()
    own, other = cell_rows(feat, fs, range(8)), cell_rows(feat_o, fs, range(8))
    for v in range(8):
        both[v] = jnp.concatenate([pick(core, own[v], other[v]), pick(core, other[v], own[v])], axis=0).astype(BF)
    select = select_ref[...]
    empty = jnp.zeros((8, 128), F32)
    for k, ref in enumerate((cot, cot_o)):
        fine_rows(ref, cs)
        planes = []
        for a in range(4):
            rows = [cs[pl.ds(a * 16 + n, 8, stride=64), :] for n in range(16)]
            ends[k, a, 0:8, :], ends[k, a, 8:16, :] = rows[0], rows[15]
            planes.append(jnp.concatenate([empty] + rows + [empty], axis=0).astype(BF))
        for p in range(4):
            cols[k, p] = columns(planes, p, select)
    chip = lambda px, py: pl.multiple_of((py * 4 + px) * 32, 32)
    near = lax.rem(x + 1 + 2 * core, 4)
    starts = (
        chip(lax.rem(x + 2, 4), either(core, row, 1 - row)),
        chip(near, 1 - row),
        chip(near, row),
    )
    for k, ref in ((1, w_o), (0, w)):
        if k == 0:
            load.wait()
        turned_weights(ref, wk, wt)
        for n, start in enumerate(starts):
            chosen[k, n * 32 : (n + 1) * 32, :] = wt[pl.ds(start, 32), :]
        for n, py in ((6, 1 - row), (7, row)):
            start = pl.multiple_of(chip(x, py) + core * 16, 16)
            chosen[k, n * 16 : (n + 1) * 16, :] = wt[pl.ds(start, 16), :]


def ready(feat, feat_o, cot, cot_o, w_o, select, w):
    return call(
        ready_body,
        (
            s((8, 32, 128)),
            s((2, 128, 512)),
            s((2, 4, 144, 512)),
            s((2, 4, 16, 128), F32),
            s((4, 4, 4, 8, 256)),
        ),
        [
            pltpu.VMEM((256, 64), F32),
            pltpu.VMEM((512, 128), F32),
            pltpu.VMEM((512, 256), BF),
            pltpu.VMEM((256, 512), BF),
            pltpu.SemaphoreType.DMA,
        ],
        (200000000, 2500000),
        in_specs=[pl.BlockSpec(memory_space=pltpu.VMEM)] * 6 + [pl.BlockSpec(memory_space=pltpu.HBM)],
    )(feat, feat_o, cot, cot_o, w_o, select, pltpu.with_memory_space_constraint(w, pltpu.HBM))


def partial_rows(chosen, tile, pair):
    total = None
    for k in range(2):
        halves = []
        for v in (2 * pair, 2 * pair + 1):
            parts = []
            for p in range(4):
                for r in range(4):
                    parts += tile(k, p, v, slice(r * 128, (r + 1) * 128))
            halves.append(jnp.concatenate(parts, axis=0))
        part = dot(chosen[k], jnp.concatenate(halves, axis=1))
        total = part if total is None else total + part
    high = total.astype(BF)
    return high, (total - high.astype(F32)).astype(BF), total


def middle_body(chosen, cols, mid, mid_away, mid_kept):
    tile = lambda k, p, v, lanes: [cols[k, p, 16 * v : 16 * v + 32, lanes]]
    for pair in (1, 2):
        high, rest, total = partial_rows(chosen, tile, pair)
        for half in range(2):
            i, lanes = 2 * pair + half - 2, slice(half * 128, (half + 1) * 128)
            mid[i], mid[4 + i] = high[0:96, lanes], rest[0:96, lanes]
            mid_away[i, 0:16, :] = high[96:112, lanes]
            mid_away[i, 16:32, :] = rest[96:112, lanes]
            mid_kept[i] = total[112:128, lanes]


def middle(chosen, cols):
    return call(
        middle_body,
        (s((8, 96, 128)), s((4, 32, 128)), s((4, 16, 128), F32)),
        [],
        (200000000, 1500000),
    )(chosen, cols)


def grad_body(
    chosen, cols, ends, select_ref, halo, halo_o, both, mid, mid_away, mid_kept, far, side_y, side, away, kept
):
    core = core_index()
    up = pick(core, halo[0:32, :].astype(F32), halo_o[0:32, :].astype(F32)).astype(BF)
    down = pick(core, halo_o[0:32, :].astype(F32), halo[0:32, :].astype(F32)).astype(BF)
    for out in (far, side_y, side, away):
        out[0], out[9] = up, down
        for v in range(8):
            out[v + 1] = both[v]
    select = select_ref[...]
    tips = {}
    for k in range(2):
        planes = []
        for a in range(4):
            mine_at, theirs_at = 32 + (k * 4 + a) * 8, 32 + ((1 - k) * 4 + a) * 8
            own, other = halo[mine_at : mine_at + 8, :].astype(F32), halo_o[theirs_at : theirs_at + 8, :].astype(F32)
            pieces = [pick(core, own, other), ends[k, a], pick(core, other, own)]
            planes.append(jnp.concatenate(pieces, axis=0).astype(BF))
        for p in range(4):
            tips[k, p] = columns(planes, p, select)

    def tile(k, p, v, lanes):
        if v == 0:
            return [tips[k, p][0:16, lanes], cols[k, p, 16:32, lanes]]
        if v == 7:
            return [cols[k, p, 112:128, lanes], tips[k, p][16:32, lanes]]
        return [cols[k, p, 16 * v : 16 * v + 32, lanes]]

    for pair in (0, 3):
        high, rest, total = partial_rows(chosen, tile, pair)
        for half in range(2):
            v, lanes = 2 * pair + half, slice(half * 128, (half + 1) * 128)
            for n, out in enumerate((far, side_y, side)):
                out[10 + v] = high[n * 32 : (n + 1) * 32, lanes]
                out[18 + v] = rest[n * 32 : (n + 1) * 32, lanes]
            away[10 + v, 0:16, :] = high[96:112, lanes]
            away[10 + v, 16:32, :] = rest[96:112, lanes]
            kept[v] = total[112:128, lanes]
    for i in range(4):
        for n, out in enumerate((far, side_y, side)):
            out[12 + i] = mid[i, n * 32 : (n + 1) * 32, :]
            out[20 + i] = mid[4 + i, n * 32 : (n + 1) * 32, :]
        away[12 + i] = mid_away[i]
        kept[2 + i] = mid_kept[i]


def grad(*args):
    whole = s((26, 32, 128))
    return call(
        grad_body,
        (whole, whole, whole, s((18, 32, 128)), s((8, 16, 128), F32)),
        [],
        (400000000, 2500000),
    )(*args)


def total_body(kept, away, *refs):
    arrived, (out, rows) = refs[:6], refs[6:]
    mine = pl.ds(pl.multiple_of(core_index() * 16, 16), 16)
    for v in range(8):
        acc = kept[v] + (away[10 + v, 0:16, :].astype(F32) + away[10 + v, 16:32, :].astype(F32))
        for ref in arrived:
            acc = acc + (ref[10 + v, mine, :].astype(F32) + ref[18 + v, mine, :].astype(F32))
        for u in range(2):
            rows[pl.ds(u * 8 + v, 16, stride=16), :] = acc[:, u * 64 : (u + 1) * 64]
    for ch in range(16):
        for u in range(2):
            out[ch, u] = rows[pl.ds(ch * 16 + u * 8, 8), :].astype(BF)


def up_body(weights, spread_ref, own, side, side_y, far, away, side_o, side_y_o, far_o, out, f, y, fine):
    x, row, core = place()
    near = lax.rem(x + 3 + 2 * core, 4)
    near_o = lax.rem(x + 5 - 2 * core, 4)
    across = lax.rem(x + 2, 4)
    flip = 1 - row
    far_row = either(core, row, flip)
    places = (
        (own, x, row),
        (away, x, flip),
        (side, near, row),
        (side_o, near_o, row),
        (side_y, near, flip),
        (side_y_o, near_o, flip),
        (far, across, far_row),
        (far_o, across, 1 - far_row),
    )
    for ref, px, py in places:
        rows = pl.ds(pl.multiple_of((py * 4 + px) * 32, 32), 32)
        for t in range(10):
            f[t, rows, :] = ref[t]
    w = weights[...]
    for t in range(5):
        y[t] = dot(w, jnp.concatenate([f[2 * t], f[2 * t + 1]], axis=1))

    def tap(p, q, r, v):
        t = v + 1
        return y[t // 2, pl.ds(((p * 4 + q) * 4 + r) * 8, 8), (t % 2) * 128 : (t % 2 + 1) * 128]

    lane = lax.broadcasted_iota(jnp.int32, (8, 128), 1)
    first_half = lane < 64
    cell = lane & 63
    spread = spread_ref[...]
    for pb in range(2):
        blocks = {0: [], 1: []}
        for n in range(8):
            pairs = ((1, n), (3, n - 1)) if pb == 0 else ((2, n), (0, n + 1))
            got = {0: [], 1: []}
            for r in range(4):
                t = [sum(tap(p, q, r, v) for q, v in pairs) for p in range(4)]
                moved = pltpu.roll(jnp.where(first_half, t[3], t[0]), 64, 1)
                got[0].append(t[1] + jnp.where(first_half, 0.0, moved))
                got[1].append(t[2] + jnp.where(first_half, moved, 0.0))
            for pa in range(2):
                t0, t1, t2, t3 = got[pa]
                even = t1 + jnp.where(cell == 0, 0.0, pltpu.roll(t3, 1, 1))
                odd = t2 + jnp.where(cell == 63, 0.0, pltpu.roll(t0, 127, 1))
                blocks[pa].append(jnp.concatenate([even, odd], axis=1))
        for pa in range(2):
            rows = dot(jnp.concatenate(blocks[pa], axis=0).astype(BF), spread)
            for n in range(8):
                for m in range(2):
                    fine[pl.ds((2 * m + pa) * 16 + 2 * n + pb, 8, stride=64), :] = rows[
                        n * 8 : (n + 1) * 8, m * 128 : (m + 1) * 128
                    ]
    for o in range(8):
        for a in range(4):
            out[o, a] = fine[pl.ds((o * 4 + a) * 16, 16), :].astype(BF)


def last_body(weights, spread, own, kept, side, side_y, far, away, side_o, side_y_o, far_o, up, grad_out, f, y, fine, rows):
    total_body(kept, away, side, side_y, far, side_o, side_y_o, far_o, grad_out, rows)
    up_body(weights, spread, own, side, side_y, far, away, side_o, side_y_o, far_o, up, f, y, fine)


def last(*args):
    return call(
        last_body,
        (s((8, 4, 16, 128)), s((16, 2, 8, 64))),
        [
            pltpu.VMEM((10, 256, 128), BF),
            pltpu.VMEM((5, 512, 256), F32),
            pltpu.VMEM((512, 128), F32),
            pltpu.VMEM((256, 64), F32),
        ],
        (400000000, 2500000),
    )(*args)


def local(features, weights, cotangent):
    tiles = lax.axis_size("space")
    chans = lax.axis_size("chan")
    at = lambda ch, sp: ch * tiles + sp
    index = lambda x, row, core: (row * 4 + x % 4) * 2 + core
    swap = [(ch, ch ^ 1) for ch in range(chans)]
    cross = []
    for ch in range(chans):
        for sp in range(tiles):
            to = sp + 1 - 2 * (ch % 2)
            if 0 <= to < tiles:
                cross.append((at(ch, sp), at(ch, to)))
    chips = [(x, row, core) for row in range(2) for x in range(4) for core in range(2)]
    beside = [(index(x, row, c), index(x + 1 - 2 * c, row, c)) for x, row, c in chips]
    beside_y = [(index(x, row, c), index(x + 1 - 2 * c, 1 - row, c)) for x, row, c in chips]
    over = [(index(x, row, c), index(x + 2, (row + c) % 2, c)) for x, row, c in chips]
    over_y = [(index(x, row, c), index(x, 1 - row, c)) for x, row, c in chips]
    send = lambda a, pairs: lax.ppermute(a, "chan", pairs)

    w_own = jnp.transpose(weights, (0, 1, 2, 4, 3))
    cot_other = send(cotangent, swap)
    feat_other = send(features, swap)
    w_other = send(w_own, swap)
    edge, feat, cot, select, spread = mine(features, cotangent)
    cot_other, feat_other, edge = lax.optimization_barrier((cot_other, feat_other, edge))
    edges = pack(feat_other, cot_other, edge)
    halo = lax.ppermute(edges, ("chan", "space"), cross)
    both, chosen, cols, ends, w_near = ready(feat, feat_other, cot, cot_other, w_other, select, w_own)
    halo_other = send(halo, swap)
    rows = middle(chosen, cols)
    far, side_y, side, away, kept = grad(chosen, cols, ends, select, halo, halo_other, both, *rows)
    own = away

    far, side_y = send(far, over), send(side_y, beside_y)
    side, away = send(side, beside), send(away, over_y)
    far_o, side_y_o, side_o = send(far, swap), send(side_y, swap), send(side, swap)
    return last(w_near.reshape(512, 256), spread, own, kept, side, side_y, far, away, side_o, side_y_o, far_o)


def solution(mesh):
    return jax.shard_map(
        local,
        mesh=mesh,
        in_specs=(
            P("chan", None, "space", None),
            P(None, None, None, None, "chan"),
            P("chan", None, "space", None),
        ),
        out_specs=(P("chan", None, "space", None), P("chan", None, "space", None)),
        check_vma=False,
    )
```

```python
import jax
import jax.numpy as jnp
from jax import lax
from jax.experimental import pallas as pl
from jax.experimental.pallas import tpu as pltpu
from jax.sharding import PartitionSpec as P

BF = jnp.bfloat16
F32 = jnp.float32


def s(shape, kind=BF):
    return jax.ShapeDtypeStruct(shape, kind)


def call(body, outs, scratch, cost, limit=12 * 1024, **kw):
    return pl.pallas_call(
        body,
        out_shape=outs,
        scratch_shapes=scratch,
        cost_estimate=pl.CostEstimate(flops=cost[0], bytes_accessed=cost[1], transcendentals=0),
        compiler_params=pltpu.CompilerParams(vmem_limit_bytes=limit * 1024),
        **kw,
    )


def dot(a, b, dims=((1,), (0,))):
    return lax.dot_general(a, b, (dims, ((), ())), preferred_element_type=F32)


def core_index():
    return lax.rem(lax.axis_index("chan"), 2)


def pick(core, zero, one):
    return jnp.where(jnp.full(zero.shape, core, jnp.int32) == 0, zero, one)


def cell_rows(feat, fs, rows):
    for ch in range(16):
        for u in range(2):
            fs[pl.ds(ch * 16 + u * 8, 8), :] = feat[ch, u].astype(F32)
    return [
        jnp.concatenate([fs[pl.ds(v, 16, stride=16), :], fs[pl.ds(8 + v, 16, stride=16), :]], axis=1)
        for v in rows
    ]


def fine_rows(cot, cs):
    for o in range(8):
        for a in range(4):
            cs[pl.ds((o * 4 + a) * 16, 16), :] = cot[o, a].astype(F32)


def edge_rows(feat, cot, fs, cs):
    core = core_index()
    first, last = cell_rows(feat, fs, (0, 7))
    fine_rows(cot, cs)
    turned = [
        pick(core, cs[pl.ds(a * 16 + 15, 8, stride=64), :], cs[pl.ds(a * 16, 8, stride=64), :]) for a in range(4)
    ]
    return pick(core, last, first), turned


def turned_weights(w, wk, out):
    for p in range(4):
        for r in range(4):
            taps = [w[p, q, r].astype(F32) for q in range(4)]
            wk[pl.ds((p * 4 + r) * 32, 32), :] = jnp.concatenate(taps, axis=0).astype(BF)
    out[...] = wk[...].T


def selection():
    i = lax.broadcasted_iota(jnp.int32, (256, 512), 0)
    j = lax.broadcasted_iota(jnp.int32, (256, 512), 1)
    want = 2 * (j & 63) + (j >> 7) - 1
    same = (i >> 7) == ((j >> 6) & 1)
    return jnp.where(((i & 127) == want) & same, 1.0, 0.0).astype(BF)


def spreading():
    i = lax.broadcasted_iota(jnp.int32, (256, 256), 0)
    j = lax.broadcasted_iota(jnp.int32, (256, 256), 1)
    return jnp.where(((j >> 7) == ((i >> 6) & 1)) & ((j & 127) == 2 * (i & 63) + (i >> 7)), 1.0, 0.0).astype(BF)


def mine_body(feat_hbm, cot_hbm, edge, feat, cot, select, spread, fs, cs, sems):
    loads = [pltpu.make_async_copy(feat_hbm, feat, sems.at[0]), pltpu.make_async_copy(cot_hbm, cot, sems.at[1])]
    for load in loads:
        load.start()
    select[...] = selection()
    spread[...] = spreading()
    for load in loads:
        load.wait()
    row, turned = edge_rows(feat, cot, fs, cs)
    edge[...] = jnp.concatenate([row] + turned, axis=0)


def mine(feat, cot):
    return call(
        mine_body,
        (s((48, 128), F32), s((16, 2, 8, 64)), s((8, 4, 16, 128)), s((256, 512)), s((256, 256))),
        [pltpu.VMEM((256, 64), F32), pltpu.VMEM((512, 128), F32), pltpu.SemaphoreType.DMA((2,))],
        (0, 1000000),
        in_specs=[pl.BlockSpec(memory_space=pltpu.HBM)] * 2,
    )(*(pltpu.with_memory_space_constraint(a, pltpu.HBM) for a in (feat, cot)))


def pack_body(feat, cot, edge, out, fs, cs):
    core = core_index()
    row, turned = edge_rows(feat, cot, fs, cs)
    own = edge[0:16, :]
    out[...] = jnp.concatenate([pick(core, own, row), pick(core, row, own), edge[16:48, :]] + turned, axis=0).astype(BF)


def pack(feat, cot, edge):
    return call(
        pack_body,
        s((96, 128)),
        [pltpu.VMEM((256, 64), F32), pltpu.VMEM((512, 128), F32)],
        (0, 600000),
    )(feat, cot, edge)


def place():
    me = lax.axis_index("chan")
    core = lax.rem(me, 2)
    return lax.rem(lax.div(me, 2), 4), lax.div(me, 8), core


def either(core, zero, one):
    return zero + core * (one - zero)


def neighbours(planes, p):
    zero = jnp.zeros_like(planes[0])
    before = planes[p - 1] if p > 0 else zero
    after = planes[p + 1] if p < 3 else zero
    return jnp.concatenate([before, after], axis=1)


def columns(planes, p, select):
    return dot(neighbours(planes, p), select).astype(BF)


def ready_body(feat, feat_o, cot, cot_o, w_o, select_ref, w_hbm, both, chosen, cols, ends, w, fs, cs, wk, wt, sem):
    load = pltpu.make_async_copy(w_hbm, w, sem)
    load.start()
    x, row, core = place()
    own, other = cell_rows(feat, fs, range(8)), cell_rows(feat_o, fs, range(8))
    for v in range(8):
        both[v] = jnp.concatenate([pick(core, own[v], other[v]), pick(core, other[v], own[v])], axis=0).astype(BF)
    select = select_ref[...]
    empty = jnp.zeros((8, 128), F32)
    for k, ref in enumerate((cot, cot_o)):
        fine_rows(ref, cs)
        planes = []
        for a in range(4):
            rows = [cs[pl.ds(a * 16 + n, 8, stride=64), :] for n in range(16)]
            ends[k, a, 0:8, :], ends[k, a, 8:16, :] = rows[0], rows[15]
            planes.append(jnp.concatenate([empty] + rows + [empty], axis=0).astype(BF))
        for p in range(4):
            cols[k, p] = columns(planes, p, select)
    chip = lambda px, py: pl.multiple_of((py * 4 + px) * 32, 32)
    near = lax.rem(x + 1 + 2 * core, 4)
    starts = (
        chip(lax.rem(x + 2, 4), either(core, row, 1 - row)),
        chip(near, 1 - row),
        chip(near, row),
    )
    for k, ref in ((1, w_o), (0, w)):
        if k == 0:
            load.wait()
        turned_weights(ref, wk, wt)
        for n, start in enumerate(starts):
            chosen[k, n * 32 : (n + 1) * 32, :] = wt[pl.ds(start, 32), :]
        for n, py in ((6, 1 - row), (7, row)):
            start = pl.multiple_of(chip(x, py) + core * 16, 16)
            chosen[k, n * 16 : (n + 1) * 16, :] = wt[pl.ds(start, 16), :]


def ready(feat, feat_o, cot, cot_o, w_o, select, w):
    return call(
        ready_body,
        (
            s((8, 32, 128)),
            s((2, 128, 512)),
            s((2, 4, 144, 512)),
            s((2, 4, 16, 128), F32),
            s((4, 4, 4, 8, 256)),
        ),
        [
            pltpu.VMEM((256, 64), F32),
            pltpu.VMEM((512, 128), F32),
            pltpu.VMEM((512, 256), BF),
            pltpu.VMEM((256, 512), BF),
            pltpu.SemaphoreType.DMA,
        ],
        (200000000, 2500000),
        in_specs=[pl.BlockSpec(memory_space=pltpu.VMEM)] * 6 + [pl.BlockSpec(memory_space=pltpu.HBM)],
    )(feat, feat_o, cot, cot_o, w_o, select, pltpu.with_memory_space_constraint(w, pltpu.HBM))


def partial_rows(chosen, tile, pair):
    total = None
    for k in range(2):
        halves = []
        for v in (2 * pair, 2 * pair + 1):
            parts = []
            for p in range(4):
                for r in range(4):
                    parts += tile(k, p, v, slice(r * 128, (r + 1) * 128))
            halves.append(jnp.concatenate(parts, axis=0))
        part = dot(chosen[k], jnp.concatenate(halves, axis=1))
        total = part if total is None else total + part
    high = total.astype(BF)
    return high, (total - high.astype(F32)).astype(BF), total


def middle_body(chosen, cols, mid, mid_away, mid_kept):
    tile = lambda k, p, v, lanes: [cols[k, p, 16 * v : 16 * v + 32, lanes]]
    for pair in (1, 2):
        high, rest, total = partial_rows(chosen, tile, pair)
        for half in range(2):
            i, lanes = 2 * pair + half - 2, slice(half * 128, (half + 1) * 128)
            mid[i], mid[4 + i] = high[0:96, lanes], rest[0:96, lanes]
            mid_away[i, 0:16, :] = high[96:112, lanes]
            mid_away[i, 16:32, :] = rest[96:112, lanes]
            mid_kept[i] = total[112:128, lanes]


def middle(chosen, cols):
    return call(
        middle_body,
        (s((8, 96, 128)), s((4, 32, 128)), s((4, 16, 128), F32)),
        [],
        (200000000, 1500000),
    )(chosen, cols)


def grad_body(
    chosen, cols, ends, select_ref, halo, halo_o, both, mid, mid_away, mid_kept, far, side_y, side, away, kept
):
    core = core_index()
    up = pick(core, halo[0:32, :].astype(F32), halo_o[0:32, :].astype(F32)).astype(BF)
    down = pick(core, halo_o[0:32, :].astype(F32), halo[0:32, :].astype(F32)).astype(BF)
    for out in (far, side_y, side, away):
        out[0], out[9] = up, down
        for v in range(8):
            out[v + 1] = both[v]
    select = select_ref[...]
    pairs = []
    for k in range(2):
        planes = []
        for a in range(4):
            mine_at, theirs_at = 32 + (k * 4 + a) * 8, 32 + ((1 - k) * 4 + a) * 8
            own, other = halo[mine_at : mine_at + 8, :].astype(F32), halo_o[theirs_at : theirs_at + 8, :].astype(F32)
            pieces = [pick(core, own, other), ends[k, a], pick(core, other, own)]
            planes.append(jnp.concatenate(pieces, axis=0).astype(BF))
        pairs += [neighbours(planes, p) for p in range(4)]
    ends_of = dot(jnp.concatenate(pairs, axis=0), select).astype(BF)
    tips = {(k, p): ends_of[(k * 4 + p) * 32 : (k * 4 + p + 1) * 32] for k in range(2) for p in range(4)}

    def tile(k, p, v, lanes):
        if v == 0:
            return [tips[k, p][0:16, lanes], cols[k, p, 16:32, lanes]]
        if v == 7:
            return [cols[k, p, 112:128, lanes], tips[k, p][16:32, lanes]]
        return [cols[k, p, 16 * v : 16 * v + 32, lanes]]

    for pair in (0, 3):
        high, rest, total = partial_rows(chosen, tile, pair)
        for half in range(2):
            v, lanes = 2 * pair + half, slice(half * 128, (half + 1) * 128)
            for n, out in enumerate((far, side_y, side)):
                out[10 + v] = high[n * 32 : (n + 1) * 32, lanes]
                out[18 + v] = rest[n * 32 : (n + 1) * 32, lanes]
            away[10 + v, 0:16, :] = high[96:112, lanes]
            away[10 + v, 16:32, :] = rest[96:112, lanes]
            kept[v] = total[112:128, lanes]
    for i in range(4):
        for n, out in enumerate((far, side_y, side)):
            out[12 + i] = mid[i, n * 32 : (n + 1) * 32, :]
            out[20 + i] = mid[4 + i, n * 32 : (n + 1) * 32, :]
        away[12 + i] = mid_away[i]
        kept[2 + i] = mid_kept[i]


def grad(*args):
    whole = s((26, 32, 128))
    return call(
        grad_body,
        (whole, whole, whole, s((18, 32, 128)), s((8, 16, 128), F32)),
        [],
        (400000000, 2500000),
    )(*args)


def total_body(kept, away, *refs):
    arrived, (out, rows) = refs[:6], refs[6:]
    mine = pl.ds(pl.multiple_of(core_index() * 16, 16), 16)
    for v in range(8):
        acc = kept[v] + (away[10 + v, 0:16, :].astype(F32) + away[10 + v, 16:32, :].astype(F32))
        for ref in arrived:
            acc = acc + (ref[10 + v, mine, :].astype(F32) + ref[18 + v, mine, :].astype(F32))
        for u in range(2):
            rows[pl.ds(u * 8 + v, 16, stride=16), :] = acc[:, u * 64 : (u + 1) * 64]
    for ch in range(16):
        for u in range(2):
            out[ch, u] = rows[pl.ds(ch * 16 + u * 8, 8), :].astype(BF)


def up_body(weights, spread_ref, own, side, side_y, far, away, side_o, side_y_o, far_o, out, f, y, fine):
    x, row, core = place()
    near = lax.rem(x + 3 + 2 * core, 4)
    near_o = lax.rem(x + 5 - 2 * core, 4)
    across = lax.rem(x + 2, 4)
    flip = 1 - row
    far_row = either(core, row, flip)
    places = (
        (own, x, row),
        (away, x, flip),
        (side, near, row),
        (side_o, near_o, row),
        (side_y, near, flip),
        (side_y_o, near_o, flip),
        (far, across, far_row),
        (far_o, across, 1 - far_row),
    )
    for ref, px, py in places:
        rows = pl.ds(pl.multiple_of((py * 4 + px) * 32, 32), 32)
        for t in range(10):
            f[t, rows, :] = ref[t]
    w = weights[...]
    for t in range(5):
        y[t] = dot(w, jnp.concatenate([f[2 * t], f[2 * t + 1]], axis=1))

    def tap(p, q, r, v):
        t = v + 1
        return y[t // 2, pl.ds(((p * 4 + q) * 4 + r) * 8, 8), (t % 2) * 128 : (t % 2 + 1) * 128]

    lane = lax.broadcasted_iota(jnp.int32, (8, 128), 1)
    first_half = lane < 64
    cell = lane & 63
    spread = spread_ref[...]
    for pb in range(2):
        blocks = {0: [], 1: []}
        for n in range(8):
            pairs = ((1, n), (3, n - 1)) if pb == 0 else ((2, n), (0, n + 1))
            got = {0: [], 1: []}
            for r in range(4):
                t = [sum(tap(p, q, r, v) for q, v in pairs) for p in range(4)]
                moved = pltpu.roll(jnp.where(first_half, t[3], t[0]), 64, 1)
                got[0].append(t[1] + jnp.where(first_half, 0.0, moved))
                got[1].append(t[2] + jnp.where(first_half, moved, 0.0))
            for pa in range(2):
                t0, t1, t2, t3 = got[pa]
                even = t1 + jnp.where(cell == 0, 0.0, pltpu.roll(t3, 1, 1))
                odd = t2 + jnp.where(cell == 63, 0.0, pltpu.roll(t0, 127, 1))
                blocks[pa].append(jnp.concatenate([even, odd], axis=1))
        for pa in range(2):
            rows = dot(jnp.concatenate(blocks[pa], axis=0).astype(BF), spread)
            for n in range(8):
                for m in range(2):
                    fine[pl.ds((2 * m + pa) * 16 + 2 * n + pb, 8, stride=64), :] = rows[
                        n * 8 : (n + 1) * 8, m * 128 : (m + 1) * 128
                    ]
    for o in range(8):
        for a in range(4):
            out[o, a] = fine[pl.ds((o * 4 + a) * 16, 16), :].astype(BF)


def last_body(weights, spread, own, kept, side, side_y, far, away, side_o, side_y_o, far_o, up, grad_out, f, y, fine, rows):
    total_body(kept, away, side, side_y, far, side_o, side_y_o, far_o, grad_out, rows)
    up_body(weights, spread, own, side, side_y, far, away, side_o, side_y_o, far_o, up, f, y, fine)


def last(*args):
    return call(
        last_body,
        (s((8, 4, 16, 128)), s((16, 2, 8, 64))),
        [
            pltpu.VMEM((10, 256, 128), BF),
            pltpu.VMEM((5, 512, 256), F32),
            pltpu.VMEM((512, 128), F32),
            pltpu.VMEM((256, 64), F32),
        ],
        (400000000, 2500000),
    )(*args)


def local(features, weights, cotangent):
    tiles = lax.axis_size("space")
    chans = lax.axis_size("chan")
    at = lambda ch, sp: ch * tiles + sp
    index = lambda x, row, core: (row * 4 + x % 4) * 2 + core
    swap = [(ch, ch ^ 1) for ch in range(chans)]
    cross = []
    for ch in range(chans):
        for sp in range(tiles):
            to = sp + 1 - 2 * (ch % 2)
            if 0 <= to < tiles:
                cross.append((at(ch, sp), at(ch, to)))
    chips = [(x, row, core) for row in range(2) for x in range(4) for core in range(2)]
    beside = [(index(x, row, c), index(x + 1 - 2 * c, row, c)) for x, row, c in chips]
    beside_y = [(index(x, row, c), index(x + 1 - 2 * c, 1 - row, c)) for x, row, c in chips]
    over = [(index(x, row, c), index(x + 2, (row + c) % 2, c)) for x, row, c in chips]
    over_y = [(index(x, row, c), index(x, 1 - row, c)) for x, row, c in chips]
    send = lambda a, pairs: lax.ppermute(a, "chan", pairs)

    w_own = jnp.transpose(weights, (0, 1, 2, 4, 3))
    cot_other = send(cotangent, swap)
    feat_other = send(features, swap)
    w_other = send(w_own, swap)
    edge, feat, cot, select, spread = mine(features, cotangent)
    cot_other, feat_other, edge = lax.optimization_barrier((cot_other, feat_other, edge))
    edges = pack(feat_other, cot_other, edge)
    halo = lax.ppermute(edges, ("chan", "space"), cross)
    both, chosen, cols, ends, w_near = ready(feat, feat_other, cot, cot_other, w_other, select, w_own)
    halo_other = send(halo, swap)
    rows = middle(chosen, cols)
    far, side_y, side, away, kept = grad(chosen, cols, ends, select, halo, halo_other, both, *rows)
    own = away

    far, side_y = send(far, over), send(side_y, beside_y)
    side, away = send(side, beside), send(away, over_y)
    far_o, side_y_o, side_o = send(far, swap), send(side_y, swap), send(side, swap)
    return last(w_near.reshape(512, 256), spread, own, kept, side, side_y, far, away, side_o, side_y_o, far_o)


def solution(mesh):
    return jax.shard_map(
        local,
        mesh=mesh,
        in_specs=(
            P("chan", None, "space", None),
            P(None, None, None, None, "chan"),
            P("chan", None, "space", None),
        ),
        out_specs=(P("chan", None, "space", None), P("chan", None, "space", None)),
        check_vma=False,
    )
```

```python
import jax
import jax.numpy as jnp
from jax import lax
from jax.experimental import pallas as pl
from jax.experimental.pallas import tpu as pltpu
from jax.sharding import PartitionSpec as P

BF = jnp.bfloat16
F32 = jnp.float32


def s(shape, kind=BF):
    return jax.ShapeDtypeStruct(shape, kind)


def call(body, outs, scratch, cost, limit=12 * 1024, **kw):
    return pl.pallas_call(
        body,
        out_shape=outs,
        scratch_shapes=scratch,
        cost_estimate=pl.CostEstimate(flops=cost[0], bytes_accessed=cost[1], transcendentals=0),
        compiler_params=pltpu.CompilerParams(vmem_limit_bytes=limit * 1024),
        **kw,
    )


def dot(a, b, dims=((1,), (0,))):
    return lax.dot_general(a, b, (dims, ((), ())), preferred_element_type=F32)


def core_index():
    return lax.rem(lax.axis_index("chan"), 2)


def pick(core, zero, one):
    return jnp.where(jnp.full(zero.shape, core, jnp.int32) == 0, zero, one)


def cell_rows(feat, fs, rows):
    for ch in range(16):
        for u in range(2):
            fs[pl.ds(ch * 16 + u * 8, 8), :] = feat[ch, u].astype(F32)
    return [
        jnp.concatenate([fs[pl.ds(v, 16, stride=16), :], fs[pl.ds(8 + v, 16, stride=16), :]], axis=1)
        for v in rows
    ]


def fine_rows(cot, cs):
    for o in range(8):
        for a in range(4):
            cs[pl.ds((o * 4 + a) * 16, 16), :] = cot[o, a].astype(F32)


def edge_rows(feat, cot, fs, cs):
    core = core_index()
    first, last = cell_rows(feat, fs, (0, 7))
    fine_rows(cot, cs)
    turned = [
        pick(core, cs[pl.ds(a * 16 + 15, 8, stride=64), :], cs[pl.ds(a * 16, 8, stride=64), :]) for a in range(4)
    ]
    return pick(core, last, first), turned


def turned_weights(w, wk, out):
    for p in range(4):
        for r in range(4):
            taps = [w[p, q, r].astype(F32) for q in range(4)]
            wk[pl.ds((p * 4 + r) * 32, 32), :] = jnp.concatenate(taps, axis=0).astype(BF)
    out[...] = wk[...].T


def selection():
    i = lax.broadcasted_iota(jnp.int32, (256, 512), 0)
    j = lax.broadcasted_iota(jnp.int32, (256, 512), 1)
    want = 2 * (j & 63) + (j >> 7) - 1
    same = (i >> 7) == ((j >> 6) & 1)
    return jnp.where(((i & 127) == want) & same, 1.0, 0.0).astype(BF)


def spreading():
    i = lax.broadcasted_iota(jnp.int32, (256, 256), 0)
    j = lax.broadcasted_iota(jnp.int32, (256, 256), 1)
    return jnp.where(((j >> 7) == ((i >> 6) & 1)) & ((j & 127) == 2 * (i & 63) + (i >> 7)), 1.0, 0.0).astype(BF)


def mine_body(feat_hbm, cot_hbm, edge, feat, cot, select, spread, fs, cs, sems):
    loads = [pltpu.make_async_copy(feat_hbm, feat, sems.at[0]), pltpu.make_async_copy(cot_hbm, cot, sems.at[1])]
    for load in loads:
        load.start()
    select[...] = selection()
    spread[...] = spreading()
    for load in loads:
        load.wait()
    row, turned = edge_rows(feat, cot, fs, cs)
    edge[...] = jnp.concatenate([row] + turned, axis=0)


def mine(feat, cot):
    return call(
        mine_body,
        (s((48, 128), F32), s((16, 2, 8, 64)), s((8, 4, 16, 128)), s((256, 512)), s((256, 256))),
        [pltpu.VMEM((256, 64), F32), pltpu.VMEM((512, 128), F32), pltpu.SemaphoreType.DMA((2,))],
        (0, 1000000),
        in_specs=[pl.BlockSpec(memory_space=pltpu.HBM)] * 2,
    )(*(pltpu.with_memory_space_constraint(a, pltpu.HBM) for a in (feat, cot)))


def pack_body(feat, cot, edge, out, fs, cs):
    core = core_index()
    row, turned = edge_rows(feat, cot, fs, cs)
    own = edge[0:16, :]
    out[...] = jnp.concatenate([pick(core, own, row), pick(core, row, own), edge[16:48, :]] + turned, axis=0).astype(BF)


def pack(feat, cot, edge):
    return call(
        pack_body,
        s((96, 128)),
        [pltpu.VMEM((256, 64), F32), pltpu.VMEM((512, 128), F32)],
        (0, 600000),
    )(feat, cot, edge)


def place():
    me = lax.axis_index("chan")
    core = lax.rem(me, 2)
    return lax.rem(lax.div(me, 2), 4), lax.div(me, 8), core


def either(core, zero, one):
    return zero + core * (one - zero)


def neighbours(planes, p):
    zero = jnp.zeros_like(planes[0])
    before = planes[p - 1] if p > 0 else zero
    after = planes[p + 1] if p < 3 else zero
    return jnp.concatenate([before, after], axis=1)


def columns(planes, p, select):
    return dot(neighbours(planes, p), select).astype(BF)


def ready_body(feat, feat_o, cot, cot_o, w_o, select_ref, w_hbm, both, chosen, cols, ends, w, fs, cs, wk, wt, sem):
    load = pltpu.make_async_copy(w_hbm, w, sem)
    load.start()
    x, row, core = place()
    own, other = cell_rows(feat, fs, range(8)), cell_rows(feat_o, fs, range(8))
    for v in range(8):
        both[v] = jnp.concatenate([pick(core, own[v], other[v]), pick(core, other[v], own[v])], axis=0).astype(BF)
    select = select_ref[...]
    empty = jnp.zeros((8, 128), F32)
    for k, ref in enumerate((cot, cot_o)):
        fine_rows(ref, cs)
        planes = []
        for a in range(4):
            rows = [cs[pl.ds(a * 16 + n, 8, stride=64), :] for n in range(16)]
            ends[k, a, 0:8, :], ends[k, a, 8:16, :] = rows[0], rows[15]
            planes.append(jnp.concatenate([empty] + rows + [empty], axis=0).astype(BF))
        for p in range(4):
            cols[k, p] = columns(planes, p, select)
    chip = lambda px, py: pl.multiple_of((py * 4 + px) * 32, 32)
    near = lax.rem(x + 1 + 2 * core, 4)
    starts = (
        chip(lax.rem(x + 2, 4), either(core, row, 1 - row)),
        chip(near, 1 - row),
        chip(near, row),
    )
    for k, ref in ((1, w_o), (0, w)):
        if k == 0:
            load.wait()
        turned_weights(ref, wk, wt)
        for n, start in enumerate(starts):
            chosen[k, n * 32 : (n + 1) * 32, :] = wt[pl.ds(start, 32), :]
        for n, py in ((6, 1 - row), (7, row)):
            start = pl.multiple_of(chip(x, py) + core * 16, 16)
            chosen[k, n * 16 : (n + 1) * 16, :] = wt[pl.ds(start, 16), :]


def ready(feat, feat_o, cot, cot_o, w_o, select, w):
    return call(
        ready_body,
        (
            s((8, 32, 128)),
            s((2, 128, 512)),
            s((2, 4, 144, 512)),
            s((2, 4, 16, 128), F32),
            s((4, 4, 4, 8, 256)),
        ),
        [
            pltpu.VMEM((256, 64), F32),
            pltpu.VMEM((512, 128), F32),
            pltpu.VMEM((512, 256), BF),
            pltpu.VMEM((256, 512), BF),
            pltpu.SemaphoreType.DMA,
        ],
        (200000000, 2500000),
        in_specs=[pl.BlockSpec(memory_space=pltpu.VMEM)] * 6 + [pl.BlockSpec(memory_space=pltpu.HBM)],
    )(feat, feat_o, cot, cot_o, w_o, select, pltpu.with_memory_space_constraint(w, pltpu.HBM))


def partial_rows(chosen, tile, pair):
    total = None
    for k in range(2):
        halves = []
        for v in (2 * pair, 2 * pair + 1):
            parts = []
            for p in range(4):
                for r in range(4):
                    parts += tile(k, p, v, slice(r * 128, (r + 1) * 128))
            halves.append(jnp.concatenate(parts, axis=0))
        part = dot(chosen[k], jnp.concatenate(halves, axis=1))
        total = part if total is None else total + part
    high = total.astype(BF)
    return high, (total - high.astype(F32)).astype(BF), total


def middle_body(chosen, cols, mid, mid_away, mid_kept):
    tile = lambda k, p, v, lanes: [cols[k, p, 16 * v : 16 * v + 32, lanes]]
    for pair in (1, 2):
        high, rest, total = partial_rows(chosen, tile, pair)
        for half in range(2):
            i, lanes = 2 * pair + half - 2, slice(half * 128, (half + 1) * 128)
            mid[i], mid[4 + i] = high[0:96, lanes], rest[0:96, lanes]
            mid_away[i, 0:16, :] = high[96:112, lanes]
            mid_away[i, 16:32, :] = rest[96:112, lanes]
            mid_kept[i] = total[112:128, lanes]


def middle(chosen, cols):
    return call(
        middle_body,
        (s((8, 96, 128)), s((4, 32, 128)), s((4, 16, 128), F32)),
        [],
        (200000000, 1500000),
    )(chosen, cols)


def grad_body(
    chosen, cols, ends, select_ref, halo, halo_o, both, mid, mid_away, mid_kept, far, side_y, side, away, kept
):
    core = core_index()
    up = pick(core, halo[0:32, :].astype(F32), halo_o[0:32, :].astype(F32)).astype(BF)
    down = pick(core, halo_o[0:32, :].astype(F32), halo[0:32, :].astype(F32)).astype(BF)
    for out in (far, side_y, side, away):
        out[0], out[9] = up, down
        for v in range(8):
            out[v + 1] = both[v]
    select = select_ref[...]
    pairs = []
    for k in range(2):
        planes = []
        for a in range(4):
            mine_at, theirs_at = 32 + (k * 4 + a) * 8, 32 + ((1 - k) * 4 + a) * 8
            own, other = halo[mine_at : mine_at + 8, :].astype(F32), halo_o[theirs_at : theirs_at + 8, :].astype(F32)
            pieces = [pick(core, own, other), ends[k, a], pick(core, other, own)]
            planes.append(jnp.concatenate(pieces, axis=0).astype(BF))
        pairs += [neighbours(planes, p) for p in range(4)]
    ends_of = dot(jnp.concatenate(pairs, axis=0), select).astype(BF)
    tips = {(k, p): ends_of[(k * 4 + p) * 32 : (k * 4 + p + 1) * 32] for k in range(2) for p in range(4)}

    def tile(k, p, v, lanes):
        if v == 0:
            return [tips[k, p][0:16, lanes], cols[k, p, 16:32, lanes]]
        if v == 7:
            return [cols[k, p, 112:128, lanes], tips[k, p][16:32, lanes]]
        return [cols[k, p, 16 * v : 16 * v + 32, lanes]]

    for pair in (0, 3):
        high, rest, total = partial_rows(chosen, tile, pair)
        for half in range(2):
            v, lanes = 2 * pair + half, slice(half * 128, (half + 1) * 128)
            for n, out in enumerate((far, side_y, side)):
                out[10 + v] = high[n * 32 : (n + 1) * 32, lanes]
                out[18 + v] = rest[n * 32 : (n + 1) * 32, lanes]
            away[10 + v, 0:16, :] = high[96:112, lanes]
            away[10 + v, 16:32, :] = rest[96:112, lanes]
            kept[v] = total[112:128, lanes]
    for i in range(4):
        for n, out in enumerate((far, side_y, side)):
            out[12 + i] = mid[i, n * 32 : (n + 1) * 32, :]
            out[20 + i] = mid[4 + i, n * 32 : (n + 1) * 32, :]
        away[12 + i] = mid_away[i]
        kept[2 + i] = mid_kept[i]


def grad(*args):
    whole = s((26, 32, 128))
    return call(
        grad_body,
        (whole, whole, whole, s((18, 32, 128)), s((8, 16, 128), F32)),
        [],
        (400000000, 2500000),
    )(*args)


def total_body(kept, away, *refs):
    arrived, (out, rows) = refs[:6], refs[6:]
    mine = pl.ds(pl.multiple_of(core_index() * 16, 16), 16)
    for v in range(8):
        acc = kept[v] + (away[10 + v, 0:16, :].astype(F32) + away[10 + v, 16:32, :].astype(F32))
        for ref in arrived:
            acc = acc + (ref[10 + v, mine, :].astype(F32) + ref[18 + v, mine, :].astype(F32))
        for u in range(2):
            rows[pl.ds(u * 8 + v, 16, stride=16), :] = acc[:, u * 64 : (u + 1) * 64]
    for ch in range(16):
        for u in range(2):
            out[ch, u] = rows[pl.ds(ch * 16 + u * 8, 8), :].astype(BF)


def up_body(weights, spread_ref, own, side, side_y, far, away, side_o, side_y_o, far_o, out, f, y, fine):
    x, row, core = place()
    near = lax.rem(x + 3 + 2 * core, 4)
    near_o = lax.rem(x + 5 - 2 * core, 4)
    across = lax.rem(x + 2, 4)
    flip = 1 - row
    far_row = either(core, row, flip)
    places = (
        (own, x, row),
        (away, x, flip),
        (side, near, row),
        (side_o, near_o, row),
        (side_y, near, flip),
        (side_y_o, near_o, flip),
        (far, across, far_row),
        (far_o, across, 1 - far_row),
    )
    for ref, px, py in places:
        rows = pl.ds(pl.multiple_of((py * 4 + px) * 32, 32), 32)
        for t in range(10):
            f[t, rows, :] = ref[t]
    w = weights[...]
    for t in range(5):
        y[t] = dot(w, jnp.concatenate([f[2 * t], f[2 * t + 1]], axis=1))

    def tap(p, q, r, v):
        t = v + 1
        return y[t // 2, pl.ds(((p * 4 + q) * 4 + r) * 8, 8), (t % 2) * 128 : (t % 2 + 1) * 128]

    lane = lax.broadcasted_iota(jnp.int32, (8, 128), 1)
    first_half = lane < 64
    cell = lane & 63
    spread = spread_ref[...]
    groups = []
    for pb in range(2):
        blocks = {0: [], 1: []}
        for n in range(8):
            pairs = ((1, n), (3, n - 1)) if pb == 0 else ((2, n), (0, n + 1))
            got = {0: [], 1: []}
            for r in range(4):
                t = [sum(tap(p, q, r, v) for q, v in pairs) for p in range(4)]
                moved = pltpu.roll(jnp.where(first_half, t[3], t[0]), 64, 1)
                got[0].append(t[1] + jnp.where(first_half, 0.0, moved))
                got[1].append(t[2] + jnp.where(first_half, moved, 0.0))
            for pa in range(2):
                t0, t1, t2, t3 = got[pa]
                even = t1 + jnp.where(cell == 0, 0.0, pltpu.roll(t3, 1, 1))
                odd = t2 + jnp.where(cell == 63, 0.0, pltpu.roll(t0, 127, 1))
                blocks[pa].append(jnp.concatenate([even, odd], axis=1))
        groups += [jnp.concatenate(blocks[pa], axis=0).astype(BF) for pa in range(2)]
    ordered = dot(jnp.concatenate(groups, axis=0), spread)
    for pb in range(2):
        for pa in range(2):
            rows = ordered[(pb * 2 + pa) * 64 : (pb * 2 + pa + 1) * 64]
            for n in range(8):
                for m in range(2):
                    fine[pl.ds((2 * m + pa) * 16 + 2 * n + pb, 8, stride=64), :] = rows[
                        n * 8 : (n + 1) * 8, m * 128 : (m + 1) * 128
                    ]
    for o in range(8):
        for a in range(4):
            out[o, a] = fine[pl.ds((o * 4 + a) * 16, 16), :].astype(BF)


def last_body(weights, spread, own, kept, side, side_y, far, away, side_o, side_y_o, far_o, up, grad_out, f, y, fine, rows):
    total_body(kept, away, side, side_y, far, side_o, side_y_o, far_o, grad_out, rows)
    up_body(weights, spread, own, side, side_y, far, away, side_o, side_y_o, far_o, up, f, y, fine)


def last(*args):
    return call(
        last_body,
        (s((8, 4, 16, 128)), s((16, 2, 8, 64))),
        [
            pltpu.VMEM((10, 256, 128), BF),
            pltpu.VMEM((5, 512, 256), F32),
            pltpu.VMEM((512, 128), F32),
            pltpu.VMEM((256, 64), F32),
        ],
        (400000000, 2500000),
    )(*args)


def local(features, weights, cotangent):
    tiles = lax.axis_size("space")
    chans = lax.axis_size("chan")
    at = lambda ch, sp: ch * tiles + sp
    index = lambda x, row, core: (row * 4 + x % 4) * 2 + core
    swap = [(ch, ch ^ 1) for ch in range(chans)]
    cross = []
    for ch in range(chans):
        for sp in range(tiles):
            to = sp + 1 - 2 * (ch % 2)
            if 0 <= to < tiles:
                cross.append((at(ch, sp), at(ch, to)))
    chips = [(x, row, core) for row in range(2) for x in range(4) for core in range(2)]
    beside = [(index(x, row, c), index(x + 1 - 2 * c, row, c)) for x, row, c in chips]
    beside_y = [(index(x, row, c), index(x + 1 - 2 * c, 1 - row, c)) for x, row, c in chips]
    over = [(index(x, row, c), index(x + 2, (row + c) % 2, c)) for x, row, c in chips]
    over_y = [(index(x, row, c), index(x, 1 - row, c)) for x, row, c in chips]
    send = lambda a, pairs: lax.ppermute(a, "chan", pairs)

    w_own = jnp.transpose(weights, (0, 1, 2, 4, 3))
    cot_other = send(cotangent, swap)
    feat_other = send(features, swap)
    w_other = send(w_own, swap)
    edge, feat, cot, select, spread = mine(features, cotangent)
    cot_other, feat_other, edge = lax.optimization_barrier((cot_other, feat_other, edge))
    edges = pack(feat_other, cot_other, edge)
    halo = lax.ppermute(edges, ("chan", "space"), cross)
    both, chosen, cols, ends, w_near = ready(feat, feat_other, cot, cot_other, w_other, select, w_own)
    halo_other = send(halo, swap)
    rows = middle(chosen, cols)
    far, side_y, side, away, kept = grad(chosen, cols, ends, select, halo, halo_other, both, *rows)
    own = away

    far, side_y = send(far, over), send(side_y, beside_y)
    side, away = send(side, beside), send(away, over_y)
    far_o, side_y_o, side_o = send(far, swap), send(side_y, swap), send(side, swap)
    return last(w_near.reshape(512, 256), spread, own, kept, side, side_y, far, away, side_o, side_y_o, far_o)


def solution(mesh):
    return jax.shard_map(
        local,
        mesh=mesh,
        in_specs=(
            P("chan", None, "space", None),
            P(None, None, None, None, "chan"),
            P("chan", None, "space", None),
        ),
        out_specs=(P("chan", None, "space", None), P("chan", None, "space", None)),
        check_vma=False,
    )
```
